256 devices in a mesh: dp: 4 (over y), expert: 64 (over x, z, core).
Axes of the slice: x: 4, y: 4, z: 8, core: 2. Of those that a mesh axis runs over, the one named last changes fastest.
Arguments:
- tokens: bfloat16 [32768, 2048], P(('dp', 'expert')), may hold values from -6 to 6
- out_grad: bfloat16 [32768, 2048], P(('dp', 'expert')), may hold values from -6 to 6
- routes: int32 [32768, 6], P(('dp', 'expert')), may hold values from 0 to 63, all different within a row; in each aligned block of 128 rows (0 to 127, 128 to 255, ...) at most 13 rows name the same one
- gate_weights: bfloat16 [32768, 6], P(('dp', 'expert')), may hold values from 0.049804688 to 0.59765625
- saved_preacts: bfloat16 [4, 64, 832, 1408], P('dp', 'expert'), may hold values from -6 to 6
- gate_up: bfloat16 [64, 2048, 1408], P('expert', 'dp'), may hold values from -0.125 to 0.125
- down_proj: bfloat16 [64, 704, 2048], P('expert', 'dp'), may hold values from -0.21875 to 0.21875
Outputs:
- grad_tokens: bfloat16 [32768, 2048], P(('dp', 'expert'))
- grad_gates: bfloat16 [32768, 6], P(('dp', 'expert'))
- grad_gate_up: float32 [64, 2048, 1408], P('expert', 'dp')
- grad_down: float32 [64, 704, 2048], P('expert', 'dp')
The draws below stay inside these ranges and needn't reach their ends.
Inputs may be any that keep to these rules, and one draw needn't show every extreme that they name: `routes`: each token names 6 different experts. Within the 128 rows of one device no expert is named by more than 13 rows, a bound that some block reaches.
All inputs are finite; a program needn't handle non-finite values.
Results may differ from the reference program's by a relative error of at most 0.0095.
Values may be sent and summed in bfloat16 or wider, within the bound.
A program may use at most 128 MiB of HBM per device.

```python
import math
import jax
import jax.numpy as jnp
import numpy as np
from jax import lax

D = 2048
FF = 704
TOP = 6
TOK_DEV = 128
EXPERTS = 64
CAP = 13
TOKENS = 32768
ROUTE_COUNT = 3072
N_DP = 4


def level_of(rng, extent, split, low, largest):
    def one(dim, blocks):
        draws = jax.random.uniform(jax.random.fold_in(jax.random.fold_in(rng, 6), dim), (blocks,), jnp.float32, low / len(split), largest / len(split))
        return jnp.repeat(jnp.exp(draws), extent[dim] // blocks).reshape((-1,) + (1,) * (len(extent) - dim - 1))

    gain = one(*split[0])
    for cut in split[1:]:
        gain = gain * one(*cut)
    return gain


def assign_block(rng, own, number, rows, count, top, most, skew):
    sequence = jax.random.permutation(rng, count)
    crowded, usual = shares(count, rows * top, most, skew, True), shares(count, rows * top, most, skew, False)
    places = jnp.arange(count)

    def named(tallies, offset_by):
        used = int((tallies > 0).sum())
        fixed = max(1, used // 4)
        shifted = fixed + (places - fixed + offset_by * (used - fixed)) % max(1, count - fixed)
        return jnp.zeros((count,), jnp.int32).at[sequence[jnp.where(places < fixed, places, shifted)]].set(jnp.asarray(tallies, jnp.int32))

    tallies = jnp.where(number % 4 == 0, named(crowded, number // 4), named(usual, number - number // 4 - 1))
    mixed = jax.random.permutation(jax.random.fold_in(own, 3), count)
    donor, receiver = mixed[0:count // 2 * 2:2], mixed[1:count // 2 * 2:2]
    margin = jnp.minimum(tallies[donor] - 1, most - tallies[receiver]) // 2
    margin = jnp.where((donor == sequence[0]) | (receiver == sequence[0]) | (tallies[receiver] == 0), 0, jnp.maximum(margin, 0))
    shifted = jax.random.randint(jax.random.fold_in(own, 4), (count // 2,), 0, 1 << 20) % (margin + 1)
    tallies = tallies.at[donor].add(-shifted).at[receiver].add(shifted)
    labels = jnp.searchsorted(jnp.cumsum(tallies), jnp.arange(rows * top), side="right").astype(jnp.int32)
    grid = labels.reshape(top, rows).T
    grid = grid[jax.random.permutation(jax.random.fold_in(own, 1), rows)]
    offset_by = jax.random.randint(jax.random.fold_in(own, 2), (rows, 1), 0, top)
    return jnp.take_along_axis(grid, (jnp.arange(top)[None, :] + offset_by) % top, axis=1)


def shares(amount, total, most, skew, full):
    loads = [(1 << 20) // math.isqrt(standing ** skew) + 1 for standing in range(1, amount + 1)]
    largest = most if full else min(most, max(-(-total // amount), total * loads[0] // sum(loads)))
    least = 1 if total - largest >= amount - 1 else 0
    counts, rest = [largest] + [least] * (amount - 1), total - largest - least * (amount - 1)
    while rest > 0:
        movable = [i for i in range(1, amount) if counts[i] < largest] or [i for i in range(1, amount) if counts[i] < most]
        mass, remaining = sum([loads[i] for i in movable]), rest
        for i in movable:
            more = min(most - counts[i], max(1, remaining * loads[i] // mass), rest)
            counts[i] = counts[i] + more
            rest = rest - more
    return np.array(counts)


def bell_draw(key, dims, scale, bound, split=(), held_as=jnp.bfloat16):
    array = jax.random.normal(key, dims, jnp.float32) * scale
    if len(split) > 0:
        array = level_of(key, dims, split, -0.22, 0.18) * array
    return jnp.clip(array, min=-bound, max=bound).astype(held_as)


def setup_inputs(seed: int = 0) -> dict:
    arg_keys = jax.random.split(jax.random.key(seed), 8)
    tokens = bell_draw(arg_keys[0], (TOKENS, D), 1.0, 6.0, ((0, 256),))
    out_grad = bell_draw(arg_keys[1], (TOKENS, D), 1.0, 6.0, ((0, 256),))
    routes_keys = jax.random.split(jax.random.fold_in(arg_keys[2], 1), TOKENS // TOK_DEV)
    routes_turns = jax.random.permutation(jax.random.fold_in(arg_keys[2], 3), TOKENS // TOK_DEV)
    routes = jax.vmap(lambda own, number: assign_block(jax.random.fold_in(arg_keys[2], 2), own, number, TOK_DEV, EXPERTS, TOP, CAP, 2))(routes_keys, routes_turns).reshape((TOKENS, TOP))
    gate_weights = jnp.clip(jnp.exp(math.log(0.59765625) - 2.4849066 * jax.random.uniform(arg_keys[3], (TOKENS, TOP), jnp.float32) ** level_of(arg_keys[3], (TOKENS, TOP), ((0, 256),), -0.2, 0.2)), 0.049804688, 0.59765625).astype(jnp.bfloat16)
    saved_preacts = bell_draw(arg_keys[4], (N_DP, EXPERTS, EXPERTS * CAP, 2 * FF), 1.0, 6.0, ((0, 4), (1, 64)))
    gate_up = bell_draw(arg_keys[5], (EXPERTS, D, 2 * FF), D ** -0.5, 0.125, ((0, 64), (1, 4)))
    down_proj = bell_draw(arg_keys[6], (EXPERTS, FF, D), FF ** -0.5, 0.21875, ((0, 64), (1, 4)))
    return {"tokens": tokens, "out_grad": out_grad, "routes": routes, "gate_weights": gate_weights, "saved_preacts": saved_preacts, "gate_up": gate_up, "down_proj": down_proj}


def find_slots(route_block, capacity):
    flat = route_block.reshape(-1).astype(jnp.int32)
    onehot = (flat[:, None] == jnp.arange(EXPERTS, dtype=jnp.int32)[None, :]).astype(jnp.int32)
    before = jnp.cumsum(onehot, axis=0) - onehot
    position = lax.optimization_barrier(jnp.sum(before * onehot, axis=1)).astype(jnp.int32)
    return (flat * capacity + position).astype(jnp.int32)

def place_rows(values, slot_index):
    owner_row = jnp.arange(TOK_DEV * TOP, dtype=jnp.int32) // TOP
    empty = jnp.zeros((EXPERTS * CAP,) + values.shape[1:], values.dtype)
    return empty.at[slot_index].set(values[owner_row])

def expert_backward(operands):
    x_rows, dy_rows, g_rows, saved_rows, weights_gate_up, weights_down = operands
    gate_pre = saved_rows[:, :FF].astype(jnp.float32)
    up_pre = saved_rows[:, FF:].astype(jnp.float32)
    sigmoid_gate = jax.nn.sigmoid(gate_pre)
    act = (gate_pre * sigmoid_gate * up_pre).astype(jnp.bfloat16)
    act_grad = jnp.dot(dy_rows, weights_down.T, preferred_element_type=jnp.float32)
    gate_grad_rows = (lax.optimization_barrier(jnp.sum(act.astype(jnp.float32) * act_grad, axis=1)) / jnp.sqrt(jnp.float32(D))).astype(jnp.bfloat16)
    scaled_grad = g_rows.astype(jnp.float32)[:, None] * act_grad
    grad_gate = scaled_grad * up_pre * sigmoid_gate * (1.0 + gate_pre * (1.0 - sigmoid_gate))
    grad_up = scaled_grad * gate_pre * sigmoid_gate
    pre_grad = jnp.concatenate([grad_gate, grad_up], axis=1).astype(jnp.bfloat16)
    scaled_dy = (g_rows.astype(jnp.float32)[:, None] * dy_rows.astype(jnp.float32)).astype(jnp.bfloat16)
    row_grad = jnp.dot(pre_grad, weights_gate_up.T, preferred_element_type=jnp.float32).astype(jnp.bfloat16)
    grad_weights_gu = jnp.dot(x_rows.T, pre_grad, preferred_element_type=jnp.float32)
    grad_weights_down = jnp.dot(act.T, scaled_dy, preferred_element_type=jnp.float32)
    return (row_grad, gate_grad_rows, grad_weights_gu, grad_weights_down)

def reference(tokens, out_grad, routes, gate_weights, saved_preacts, gate_up, down_proj):
    tok_blocks = tokens.reshape(N_DP, EXPERTS, TOK_DEV, D)
    grad_blocks = out_grad.reshape(N_DP, EXPERTS, TOK_DEV, D)
    route_blocks = routes.reshape(N_DP, EXPERTS, TOK_DEV, TOP)
    gate_blocks = gate_weights.reshape(N_DP, EXPERTS, TOK_DEV * TOP)
    total_gu = jnp.zeros((EXPERTS, D, 2 * FF), jnp.float32)
    total_down = jnp.zeros((EXPERTS, FF, D), jnp.float32)
    token_grads = []
    gate_grads = []
    for replica in range(N_DP):
        slot_index = jax.vmap(lambda blk: find_slots(blk, CAP))(route_blocks[replica])
        send_x = jax.vmap(place_rows)(tok_blocks[replica], slot_index)
        send_dy = jax.vmap(place_rows)(grad_blocks[replica], slot_index)
        send_g = jax.vmap(lambda vals, idx: jnp.zeros((EXPERTS * CAP,), vals.dtype).at[idx].set(vals))(gate_blocks[replica], slot_index)
        recv_x = send_x.reshape(EXPERTS, EXPERTS, CAP, D).transpose(1, 0, 2, 3).reshape(EXPERTS, EXPERTS * CAP, D)
        recv_dy = send_dy.reshape(EXPERTS, EXPERTS, CAP, D).transpose(1, 0, 2, 3).reshape(EXPERTS, EXPERTS * CAP, D)
        recv_g = send_g.reshape(EXPERTS, EXPERTS, CAP).transpose(1, 0, 2).reshape(EXPERTS, EXPERTS * CAP)
        row_grad, gate_grad_rows, grad_gu, grad_dn = lax.map(expert_backward, (recv_x, recv_dy, recv_g, saved_preacts[replica], gate_up, down_proj))
        total_gu = total_gu + grad_gu
        total_down = total_down + grad_dn
        back_rows = row_grad.reshape(EXPERTS, EXPERTS, CAP, D).transpose(1, 0, 2, 3).reshape(EXPERTS, EXPERTS * CAP, D)
        back_gate = gate_grad_rows.reshape(EXPERTS, EXPERTS, CAP).transpose(1, 0, 2).reshape(EXPERTS, EXPERTS * CAP)

        def collect(rows_back, gates_back, idx):
            picked = rows_back[idx].astype(jnp.float32).reshape(TOK_DEV, TOP, D)
            return (lax.optimization_barrier(jnp.sum(picked, axis=1)).astype(jnp.bfloat16), gates_back[idx].reshape(TOK_DEV, TOP))
        tok_grad, gate_grad = jax.vmap(collect)(back_rows, back_gate, slot_index)
        token_grads.append(tok_grad.reshape(EXPERTS * TOK_DEV, D))
        gate_grads.append(gate_grad.reshape(EXPERTS * TOK_DEV, TOP))
    grad_scale = 1.0 / jnp.sqrt(jnp.float32(ROUTE_COUNT))
    grad_tokens = jnp.concatenate(token_grads, axis=0)
    grad_gates = jnp.concatenate(gate_grads, axis=0)
    return (grad_tokens, grad_gates, total_gu * grad_scale, total_down * grad_scale)
```

```python
import functools

import jax
import jax.numpy as jnp
from jax import lax
from jax.experimental import pallas as pl
from jax.experimental.pallas import tpu as pltpu
from jax.sharding import PartitionSpec as P

MESH = pl.DeviceIdType.MESH
BF16, F32 = jnp.bfloat16, jnp.float32
NX, NZ, NC = 4, 8, 2
PEERS = NX * NC
LANES = 128
GATE_LANE = 8


def place():
    e = lax.axis_index("expert")
    return e // (NZ * NC), lax.rem(e // NC, NZ), lax.rem(e, NC)


def device(x, z, c):
    return (lax.axis_index("dp"), (x * NZ + z) * NC + c)


def enter(x, z, c):
    barrier = pltpu.get_barrier_semaphore()
    for step in (1, NZ - 1):
        pl.semaphore_signal(barrier, inc=1, device_id=device(x, lax.rem(z + step, NZ), c), device_id_type=MESH)
    me = x * NC + c
    for step in range(1, PEERS):
        peer = lax.rem(me + step, PEERS)
        pl.semaphore_signal(barrier, inc=1, device_id=device(peer // NC, z, lax.rem(peer, NC)), device_id_type=MESH)
    pl.semaphore_wait(barrier, 2 + PEERS - 1)


def chunks_of(widths, first):
    out, spans = [], first
    for group, ws in enumerate(widths):
        col = 0
        for n, w in enumerate(ws):
            segments, off = [], 0
            for array, extra in spans[group] if n == 0 else ():
                segments.append((array, 0, extra, 0))
                off = extra
            segments.append((first["main"][group], col, w, off))
            col += w
            out.append((segments, off + w))
    return out


def dispatch_kernel(chunks, cap, side_ref, dy_ref, x_ref, side_out, dy_out, x_out, gathered_out, *scratch):
    n = len(chunks)
    ring, stage = scratch[:n], scratch[n : 2 * n]
    pick, z_send, z_recv, x_send, x_recv, own_sem, out_sem = scratch[2 * n :]
    ins, outs = (side_ref, dy_ref, x_ref), (side_out, dy_out, x_out)
    x, z, c = place()
    me = x * NC + c
    tok = dy_ref.shape[0]
    half_rows = tok // 2
    block = pick.shape[1]
    sends = NZ - 1

    for (segments, _), buf in zip(chunks, ring):
        for array, col, w, off in segments:
            buf[z, :, off : off + w] = ins[array][:, col : col + w]
    enter(x, z, c)

    def hop(ch, way, i):
        step = 1 if way == 0 else NZ - 1
        dist = i // 2
        half = lax.rem(i + way, 2)
        blk = lax.rem(z + (NZ - step) * dist, NZ)
        view = ring[ch].at[blk, pl.ds(pl.multiple_of(half * half_rows, half_rows), half_rows), :]
        return pltpu.make_async_remote_copy(
            src_ref=view,
            dst_ref=view,
            send_sem=z_send.at[ch, way, i],
            recv_sem=z_recv.at[ch, way, i],
            device_id=device(x, lax.rem(z + step, NZ), c),
            device_id_type=MESH,
        )

    def z_start(ch, i):
        for way in (0, 1):
            hop(ch, way, i).start()

    def z_arrived(ch, i):
        for way in (0, 1):
            hop(ch, way, i).wait_recv()

    def x_copies(ch, peer, slot, own):
        segments, _ = chunks[ch]
        made = []
        for array, col, w, off in segments:
            src = stage[ch].at[peer, :, off : off + w]
            dst = outs[array].at[slot, :, col : col + w]
            sem = (ch, slot if own is None else own, 0 if array == 0 else 1)
            made.append((src, dst, array))
        return made

    def x_send_copy(ch, peer):
        out = []
        for src, dst, array in x_copies(ch, peer, me, None):
            kind = 0 if array == 0 else 1
            out.append(
                pltpu.make_async_remote_copy(
                    src_ref=src,
                    dst_ref=dst,
                    send_sem=x_send.at[ch, kind, peer],
                    recv_sem=x_recv.at[ch, kind, me],
                    device_id=device(peer // NC, z, lax.rem(peer, NC)),
                    device_id_type=MESH,
                )
            )
        return out

    def x_recv_copy(ch, peer):
        out = []
        for src, dst, array in x_copies(ch, peer, peer, None):
            kind = 0 if array == 0 else 1
            out.append(
                pltpu.make_async_remote_copy(
                    src_ref=src,
                    dst_ref=dst,
                    send_sem=x_send.at[ch, kind, peer],
                    recv_sem=x_recv.at[ch, kind, peer],
                    device_id=device(peer // NC, z, lax.rem(peer, NC)),
                    device_id_type=MESH,
                )
            )
        return out

    def own_copy(ch):
        return [
            pltpu.make_async_copy(src, dst, own_sem.at[ch, 0 if array == 0 else 1])
            for src, dst, array in x_copies(ch, me, me, None)
        ]

    def make_pick():
        lane = lax.broadcasted_iota(jnp.int32, (LANES, tok), 0)
        eye = (lax.broadcasted_iota(jnp.int32, (LANES, LANES), 0) == lax.broadcasted_iota(jnp.int32, (LANES, LANES), 1)).astype(BF16)
        earlier = (
            lax.broadcasted_iota(jnp.int32, (tok, tok), 0) < lax.broadcasted_iota(jnp.int32, (tok, tok), 1)
        ).astype(BF16)
        slot_row = lax.broadcasted_iota(jnp.int32, (block, tok), 0).astype(F32)
        peer_row = lax.broadcasted_iota(jnp.int32, (PEERS, tok), 0)
        expert_row = ((peer_row // NC) * (NZ * NC) + z * NC + lax.rem(peer_row, NC)).astype(F32)
        del lane

        def one(s, _):
            side = ring[0][s, :, 0:LANES]
            turned = lax.dot_general(eye, side, (((1,), (1,)), ((), ())), preferred_element_type=F32)
            match = jnp.zeros((PEERS, tok), F32)
            for k in range(6):
                match = match + (jnp.broadcast_to(turned[k : k + 1, :], (PEERS, tok)) == expert_row).astype(F32)
            position = jnp.dot(match.astype(BF16), earlier, preferred_element_type=F32)
            slot = jnp.where(match > 0.0, position + (s * cap).astype(F32), -1.0)
            for peer in range(PEERS):
                hit = jnp.broadcast_to(slot[peer : peer + 1, :], (block, tok)) == slot_row
                pick[peer, :, pl.ds(pl.multiple_of(s * tok, tok), tok)] = hit.astype(F32).astype(BF16)
            return 0

        lax.fori_loop(0, NZ, one, 0)

    def piece(ch, peer):
        width = chunks[ch][1]
        rows = pick[peer]
        for lo in range(0, width, 256):
            w = min(256, width - lo)
            cols = ring[ch][:, :, lo : lo + w].reshape(NZ * tok, w)
            stage[ch][peer, :, lo : lo + w] = jnp.dot(rows, cols, preferred_element_type=F32).astype(BF16)

        @pl.when(peer != me)
        def _():
            for copy in x_send_copy(ch, peer):
                copy.start()

        @pl.when(peer == me)
        def _():
            for copy in own_copy(ch):
                copy.start()

    def pieces(ch, lo, hi):
        def one(peer, _):
            piece(ch, peer)
            return 0

        lax.fori_loop(lo, hi, one, 0)

    ticks = sends - 2
    for ch in range(n):
        z_start(ch, 0)
        z_start(ch, 1)
        if ch > 0:
            z_arrived(ch - 1, sends - 2)
            z_arrived(ch - 1, sends - 1)
            if ch == 1:
                make_pick()

        def tick(i, _, ch=ch):
            z_arrived(ch, i)
            z_start(ch, i + 2)
            if ch > 0:
                pieces(ch - 1, (PEERS * i) // ticks, (PEERS * (i + 1)) // ticks)
            return 0

        lax.fori_loop(0, ticks, tick, 0)
    z_arrived(n - 1, sends - 2)
    z_arrived(n - 1, sends - 1)
    if n == 1:
        make_pick()
    pieces(n - 1, 0, PEERS)
    keep = pltpu.make_async_copy(ring[0].at[:, :, 0:LANES], gathered_out, out_sem)
    keep.start()
    for ch in range(n):

        def finish(i, _, ch=ch):
            for way in (0, 1):
                hop(ch, way, i).wait_send()
            return 0

        lax.fori_loop(0, sends, finish, 0)

        def arrive(step, _, ch=ch):
            peer = lax.rem(me + step, PEERS)
            for copy in x_recv_copy(ch, peer):
                copy.wait_recv()
            for copy in x_send_copy(ch, peer):
                copy.wait_send()
            return 0

        lax.fori_loop(1, PEERS, arrive, 0)
        for copy in own_copy(ch):
            copy.wait()
    keep.wait()


def dispatch(side, dy, x, cap):
    tok, width = dy.shape
    block = NZ * cap
    parts = {0: [(0, LANES)], 1: [], "main": (1, 2)}
    chunks = chunks_of(([width // 2] * 2, [width // 2] * 2), parts)
    n = len(chunks)
    vmem = pl.BlockSpec(memory_space=pltpu.VMEM)
    anywhere = pl.BlockSpec(memory_space=pl.ANY)
    return pl.pallas_call(
        functools.partial(dispatch_kernel, chunks, cap),
        out_shape=(
            jax.ShapeDtypeStruct((PEERS, block, LANES), BF16),
            jax.ShapeDtypeStruct((PEERS, block, width), BF16),
            jax.ShapeDtypeStruct((PEERS, block, width), BF16),
            jax.ShapeDtypeStruct((NZ, tok, LANES), BF16),
        ),
        in_specs=[vmem] * 3,
        out_specs=(anywhere,) * 4,
        scratch_shapes=[pltpu.VMEM((NZ, tok, w), BF16) for _, w in chunks]
        + [pltpu.VMEM((PEERS, block, w), BF16) for _, w in chunks]
        + [
            pltpu.VMEM((PEERS, block, NZ * tok), BF16),
            pltpu.SemaphoreType.DMA((n, 2, NZ - 1)),
            pltpu.SemaphoreType.DMA((n, 2, NZ - 1)),
            pltpu.SemaphoreType.DMA((n, 2, PEERS)),
            pltpu.SemaphoreType.DMA((n, 2, PEERS)),
            pltpu.SemaphoreType.DMA((n, 2)),
            pltpu.SemaphoreType.DMA,
        ],
        compiler_params=pltpu.CompilerParams(collective_id=0, has_side_effects=True, vmem_limit_bytes=48 << 20),
        cost_estimate=pl.CostEstimate(flops=8_000_000_000, bytes_accessed=250_000_000, transcendentals=0),
        name="dispatch",
    )(side, dy, x)


def give_back_kernel(chunks, cap, side_ref, gate_ref, row_ref, gate_out, tok_out, *scratch):
    n = len(chunks)
    landed, total, leave, come = (scratch[k * n : (k + 1) * n] for k in range(4))
    spread, z_send, z_recv, x_send, x_recv, own_sem = scratch[4 * n :]
    ins, outs = (gate_ref, row_ref), (gate_out, tok_out)
    x, z, c = place()
    me = x * NC + c
    tok = tok_out.shape[0]
    half_rows = tok // 2
    block = row_ref.shape[1]
    pad = landed[0].shape[1]
    sends = NZ - 1

    for buf, (_, w) in zip(landed, chunks):
        buf[:, block:, :] = jnp.zeros((PEERS, pad - block, w), BF16)
    enter(x, z, c)

    def x_copies(ch, src_slot, dst_slot, sem_slot, peer):
        made = []
        for array, col, w, off in chunks[ch][0]:
            made.append(
                pltpu.make_async_remote_copy(
                    src_ref=ins[array].at[src_slot, :, col : col + w],
                    dst_ref=landed[ch].at[dst_slot, 0:block, off : off + w],
                    send_sem=x_send.at[ch, array, peer],
                    recv_sem=x_recv.at[ch, array, sem_slot],
                    device_id=device(peer // NC, z, lax.rem(peer, NC)),
                    device_id_type=MESH,
                )
            )
        return made

    def own_copy(ch):
        return [
            pltpu.make_async_copy(
                ins[array].at[me, :, col : col + w], landed[ch].at[me, 0:block, off : off + w], own_sem.at[ch, array]
            )
            for array, col, w, off in chunks[ch][0]
        ]

    for ch in range(n):

        def send(step, _, ch=ch):
            peer = lax.rem(me + step, PEERS)
            for copy in x_copies(ch, peer, me, me, peer):
                copy.start()
            return 0

        lax.fori_loop(1, PEERS, send, 0)
        for copy in own_copy(ch):
            copy.start()

    later = (
        lax.broadcasted_iota(jnp.int32, (tok, tok), 1) < lax.broadcasted_iota(jnp.int32, (tok, tok), 0)
    ).astype(BF16)
    lane = lax.broadcasted_iota(jnp.int32, (tok, LANES), 1)
    expert_lane = jnp.where(lane < PEERS, (lane // NC) * (NZ * NC) + z * NC + lax.rem(lane, NC), -1).astype(F32)
    slot_lane = lax.broadcasted_iota(jnp.int32, (tok, pad), 1).astype(F32)

    def spread_one(s, _):
        side = side_ref[s].astype(F32)
        match = jnp.zeros((tok, LANES), F32)
        for k in range(6):
            match = match + (jnp.broadcast_to(side[:, k : k + 1], (tok, LANES)) == expert_lane).astype(F32)
        position = jnp.dot(later, match.astype(BF16), preferred_element_type=F32)
        slot = jnp.where(match > 0.0, position + (s * cap).astype(F32), -1.0)
        for peer in range(PEERS):
            hit = jnp.broadcast_to(slot[:, peer : peer + 1], (tok, pad)) == slot_lane
            spread[s, :, peer * pad : (peer + 1) * pad] = hit.astype(F32).astype(BF16)
        return 0

    lax.fori_loop(0, NZ, spread_one, 0)

    def x_arrived(ch):
        def one(step, _):
            peer = lax.rem(me + step, PEERS)
            for copy in x_copies(ch, peer, peer, peer, peer):
                copy.wait_recv()
            return 0

        lax.fori_loop(1, PEERS, one, 0)
        for copy in own_copy(ch):
            copy.wait()

    def combine(ch, k):
        width = chunks[ch][1]
        s = lax.rem(z + NZ // 2 + k, NZ)
        rows = spread[s]
        for lo in range(0, width, 256):
            w = min(256, width - lo)
            cols = landed[ch][:, :, lo : lo + w].reshape(PEERS * pad, w)
            total[ch][s, :, lo : lo + w] = jnp.dot(rows, cols, preferred_element_type=F32)

    def combines(ch, lo, hi):
        def one(k, _):
            combine(ch, k)
            return 0

        lax.fori_loop(lo, hi, one, 0)

    def hop(ch, way, i):
        step = 1 if way == 0 else NZ - 1
        return pltpu.make_async_remote_copy(
            src_ref=leave[ch].at[way, i],
            dst_ref=come[ch].at[way, i],
            send_sem=z_send.at[ch, way, i],
            recv_sem=z_recv.at[ch, way, i],
            device_id=device(x, lax.rem(z + step, NZ), c),
            device_id_type=MESH,
        )

    def part(ch, way, i):
        step = 1 if way == 0 else NZ - 1
        dist = NZ // 2 - (i + 1) // 2
        half = lax.rem(i + way, 2)
        s = lax.rem(z + step * dist, NZ)
        return total[ch][s, pl.ds(pl.multiple_of(half * half_rows, half_rows), half_rows), :]

    def z_step(ch, i, first):
        for way in (0, 1):
            value = part(ch, way, i)
            if not first:
                hop(ch, way, i - 2).wait_recv()
                value = value + come[ch][way, i - 2].astype(F32)
            leave[ch][way, i] = value.astype(BF16)
            hop(ch, way, i).start()

    def finish(ch):
        for way in (0, 1):
            hop(ch, way, sends - 2).wait_recv()
            hop(ch, way, sends - 1).wait_recv()
        for half in (0, 1):
            rows = slice(half * half_rows, (half + 1) * half_rows)
            value = total[ch][z, rows, :]
            for way in (0, 1):
                i = sends - 1 if (sends - 1 + way) % 2 == half else sends - 2
                value = value + come[ch][way, i].astype(F32)
            for array, col, w, off in chunks[ch][0]:
                outs[array][rows, col : col + w] = value[:, off : off + w].astype(BF16)

    x_arrived(0)
    combines(0, 0, NZ)
    ticks = sends - 2
    for ch in range(n):
        z_step(ch, 0, True)
        z_step(ch, 1, True)
        if ch > 0:
            finish(ch - 1)
        if ch + 1 < n:
            x_arrived(ch + 1)

        def tick(i, _, ch=ch):
            z_step(ch, i + 2, False)
            if ch + 1 < n:
                combines(ch + 1, (NZ * i) // ticks, (NZ * (i + 1)) // ticks)
            return 0

        lax.fori_loop(0, ticks, tick, 0)
    finish(n - 1)
    for ch in range(n):

        def drain(i, _, ch=ch):
            for way in (0, 1):
                hop(ch, way, i).wait_send()
            return 0

        lax.fori_loop(0, sends, drain, 0)

        def sent(step, _, ch=ch):
            peer = lax.rem(me + step, PEERS)
            for copy in x_copies(ch, peer, me, me, peer):
                copy.wait_send()
            return 0

        lax.fori_loop(1, PEERS, sent, 0)


def give_back(side, gate_rows, rows, cap):
    block, width = rows.shape[1:]
    tok = side.shape[1]
    pad = -(-block // LANES) * LANES
    parts = {0: [(0, LANES)], "main": (1,)}
    chunks = chunks_of(([width // 4] * 4,), parts)
    n = len(chunks)
    vmem = pl.BlockSpec(memory_space=pltpu.VMEM)
    return pl.pallas_call(
        functools.partial(give_back_kernel, chunks, cap),
        out_shape=(jax.ShapeDtypeStruct((tok, LANES), BF16), jax.ShapeDtypeStruct((tok, width), BF16)),
        in_specs=[vmem, vmem, vmem],
        out_specs=(vmem, vmem),
        scratch_shapes=[pltpu.VMEM((PEERS, pad, w), BF16) for _, w in chunks]
        + [pltpu.VMEM((NZ, tok, w), F32) for _, w in chunks]
        + [pltpu.VMEM((2, NZ - 1, tok // 2, w), BF16) for _, w in chunks] * 2
        + [
            pltpu.VMEM((NZ, tok, PEERS * pad), BF16),
            pltpu.SemaphoreType.DMA((n, 2, NZ - 1)),
            pltpu.SemaphoreType.DMA((n, 2, NZ - 1)),
            pltpu.SemaphoreType.DMA((n, 2, PEERS)),
            pltpu.SemaphoreType.DMA((n, 2, PEERS)),
            pltpu.SemaphoreType.DMA((n, 2)),
        ],
        compiler_params=pltpu.CompilerParams(collective_id=1, has_side_effects=True, vmem_limit_bytes=48 << 20),
        cost_estimate=pl.CostEstimate(flops=5_000_000_000, bytes_accessed=170_000_000, transcendentals=0),
        name="give_back",
    )(side, gate_rows, rows)


def on_device(tokens, out_grad, routes, gate_weights, saved_preacts, gate_up, down_proj):
    experts = lax.axis_size("expert")
    groups = lax.axis_size("dp")
    tok_rows, top = routes.shape
    width = tokens.shape[1]
    slot_total = saved_preacts.shape[2]
    cap = slot_total // experts
    hidden = saved_preacts.shape[3] // 2
    lane = lax.broadcasted_iota(jnp.int32, (tok_rows, LANES), 1)
    side = jnp.zeros((tok_rows, LANES), BF16)
    for k in range(top):
        side = jnp.where(lane == k, routes[:, k : k + 1].astype(BF16), side)
        side = jnp.where(lane == GATE_LANE + k, gate_weights[:, k : k + 1], side)
    down = lax.all_gather(down_proj[0], "dp", axis=0, tiled=True)
    up = lax.all_gather(gate_up[0], "dp", axis=0, tiled=True)
    side_rows, dy_rows, x_rows, sides = dispatch(side, out_grad, tokens, cap)

    per_x = NZ * NC * cap
    new = lax.broadcasted_iota(jnp.int32, (per_x, per_x), 0)
    old = lax.broadcasted_iota(jnp.int32, (per_x, per_x), 1)
    core, zed, p = new // (NZ * cap), (new // cap) % NZ, new % cap
    order = (old == (zed * NC + core) * cap + p).astype(BF16)
    saved_rows = (
        jnp.einsum("ij,xjf->xif", order, saved_preacts[0, 0].reshape(NX, per_x, 2 * hidden), preferred_element_type=F32)
        .astype(BF16)
        .reshape(slot_total, 2 * hidden)
    )
    side_rows = side_rows.reshape(slot_total, LANES)
    dy_rows = dy_rows.reshape(slot_total, width)
    x_rows = x_rows.reshape(slot_total, width)
    mine = side_rows[:, :top] == lax.axis_index("expert").astype(BF16)
    g_rows = jnp.sum(
        jnp.where(mine, side_rows[:, GATE_LANE : GATE_LANE + top], 0).astype(F32), axis=1, keepdims=True
    )
    gate_pre = saved_rows[:, :hidden].astype(F32)
    up_pre = saved_rows[:, hidden:].astype(F32)
    sigmoid_gate = jax.nn.sigmoid(gate_pre)
    act = (gate_pre * sigmoid_gate * up_pre).astype(BF16)
    act_grad = lax.dot_general(dy_rows, down, (((1,), (1,)), ((), ())), preferred_element_type=F32)
    gate_grad_rows = (jnp.sum(act.astype(F32) * act_grad, axis=1, keepdims=True) / jnp.sqrt(F32(width))).astype(BF16)
    scaled_grad = g_rows * act_grad
    grad_gate = scaled_grad * up_pre * sigmoid_gate * (1.0 + gate_pre * (1.0 - sigmoid_gate))
    grad_up = scaled_grad * gate_pre * sigmoid_gate
    pre_grad = jnp.concatenate([grad_gate, grad_up], axis=1).astype(BF16)
    scaled_dy = (g_rows * dy_rows.astype(F32)).astype(BF16)
    row_grad = lax.dot_general(pre_grad, up, (((1,), (1,)), ((), ())), preferred_element_type=F32).astype(BF16)
    row_lane = lax.broadcasted_iota(jnp.int32, (slot_total, LANES), 1)
    own = (row_lane < top) & (side_rows == lax.axis_index("expert").astype(BF16))
    gate_back = jnp.where(own, gate_grad_rows, 0).astype(BF16)
    gates, grad_tokens = give_back(
        sides, gate_back.reshape(PEERS, -1, LANES), row_grad.reshape(PEERS, -1, width), cap
    )
    grad_scale = 1.0 / jnp.sqrt(F32(groups * tok_rows * top))
    grad_gu = lax.psum_scatter(
        lax.dot_general(x_rows, pre_grad, (((0,), (0,)), ((), ())), preferred_element_type=F32).astype(BF16),
        "dp",
        scatter_dimension=0,
        tiled=True,
    ).astype(F32)
    grad_dn = lax.psum_scatter(
        lax.dot_general(act, scaled_dy, (((0,), (0,)), ((), ())), preferred_element_type=F32).astype(BF16),
        "dp",
        scatter_dimension=0,
        tiled=True,
    ).astype(F32)
    return (grad_tokens, gates[:, :top], (grad_gu * grad_scale)[None], (grad_dn * grad_scale)[None])


def solution(mesh):
    in_specs = (
        P(("dp", "expert"), None),
        P(("dp", "expert"), None),
        P(("dp", "expert"), None),
        P(("dp", "expert"), None),
        P("dp", "expert", None, None),
        P("expert", "dp", None),
        P("expert", "dp", None),
    )
    out_specs = (
        P(("dp", "expert"), None),
        P(("dp", "expert"), None),
        P("expert", "dp", None),
        P("expert", "dp", None),
    )
    return jax.shard_map(
        on_device, mesh=mesh, in_specs=in_specs, out_specs=out_specs, check_vma=False
    )
```

```python
import functools

import jax
import jax.numpy as jnp
from jax import lax
from jax.experimental import pallas as pl
from jax.experimental.pallas import tpu as pltpu
from jax.sharding import PartitionSpec as P

MESH = pl.DeviceIdType.MESH
BF16, F32 = jnp.bfloat16, jnp.float32
NX, NZ, NC = 4, 8, 2
NY = 4
PEERS = NX * NC
LANES = 128
TOP = 6
GATE_LANE = 8
NT = (((1,), (1,)), ((), ()))
TN = (((0,), (0,)), ((), ()))


def place():
    e = lax.axis_index("expert")
    return e // (NZ * NC), lax.rem(e // NC, NZ), lax.rem(e, NC)


def device(x, z, c):
    return (lax.axis_index("dp"), (x * NZ + z) * NC + c)


def along_y(step):
    return (lax.rem(lax.axis_index("dp") + step, NY), lax.axis_index("expert"))


def enter(x, z, c):
    barrier = pltpu.get_barrier_semaphore()
    for step in (1, NZ - 1):
        pl.semaphore_signal(barrier, inc=1, device_id=device(x, lax.rem(z + step, NZ), c), device_id_type=MESH)
    for step in (1, NY - 1):
        pl.semaphore_signal(barrier, inc=1, device_id=along_y(step), device_id_type=MESH)
    me = x * NC + c
    for step in range(1, PEERS):
        peer = lax.rem(me + step, PEERS)
        pl.semaphore_signal(barrier, inc=1, device_id=device(peer // NC, z, lax.rem(peer, NC)), device_id_type=MESH)
    pl.semaphore_wait(barrier, 2 + 2 + PEERS - 1)


def aligned(index, size):
    return pl.ds(pl.multiple_of(index * size, size), size)


def front_kernel(
    chunks,
    cap,
    side_in,
    dy_in,
    x_in,
    saved,
    up_in,
    down_in,
    side_out,
    x_out,
    pre_out,
    gate_out,
    row_out,
    dn_out,
    *scratch,
):
    n = len(chunks)
    ring, stage = scratch[:n], scratch[n : 2 * n]
    (side_own, side_rows, dy_rows, pick, up, down, act, turned_act, coef_gate, coef_up) = scratch[2 * n : 2 * n + 10]
    z_send, z_recv, x_send, x_recv, own_sem, y_send, y_recv, y_own = scratch[2 * n + 10 :]
    ins, outs = (side_own, dy_in, x_in), (side_rows, dy_rows, x_out)
    x, z, c = place()
    y = lax.axis_index("dp")
    expert = lax.axis_index("expert")
    me = x * NC + c
    tok, width = dy_in.shape
    half_rows = tok // 2
    block = pick.shape[1]
    padded = dy_rows.shape[1]
    hidden = act.shape[1]
    sends = NZ - 1
    unit = NC * padded

    eye = (lax.broadcasted_iota(jnp.int32, (tok, tok), 0) == lax.broadcasted_iota(jnp.int32, (tok, tok), 1)).astype(BF16)
    side_own[...] = lax.dot_general(eye, side_in[...], NT, preferred_element_type=F32).astype(BF16)
    for segments, buf in ((s, b) for (s, _), b in zip(chunks, ring)):
        for array, col, w, off in segments:
            buf[z, :, off : off + w] = ins[array][:, col : col + w]
    for buf in outs:
        buf[:, block:, :] = jnp.zeros((PEERS, padded - block, buf.shape[2]), BF16)
    enter(x, z, c)

    weights = ((down_in, down), (up_in, up))

    def y_copy(k, hop):
        source, whole = weights[k]
        rows = whole.shape[1]
        cut = rows // 32 * 16
        first, second = (0, cut), (cut, rows - cut)
        lo, size = (first, second, second, first, first, second)[hop]
        step = 1 if hop in (0, 1, 4) else NY - 1
        back = NY - step
        slot = y if hop < 4 else lax.rem(y + back, NY)
        src = source.at[lo : lo + size, :] if hop < 4 else whole.at[slot, lo : lo + size, :]
        return pltpu.make_async_remote_copy(
            src_ref=src,
            dst_ref=whole.at[slot, lo : lo + size, :],
            send_sem=y_send.at[k, hop],
            recv_sem=y_recv.at[k, hop],
            device_id=along_y(step),
            device_id_type=MESH,
        )

    def y_own_copy(k):
        return pltpu.make_async_copy(weights[k][0], weights[k][1].at[y], y_own.at[k])

    def y_forward(k):
        y_copy(k, 0).wait_recv()
        y_copy(k, 4).start()
        y_copy(k, 2).wait_recv()
        y_copy(k, 5).start()

    def y_arrived(k):
        for hop in (1, 3, 4, 5):
            y_copy(k, hop).wait_recv()
        y_own_copy(k).wait()

    def hop(ch, way, i):
        step = 1 if way == 0 else NZ - 1
        dist = i // 2
        half = lax.rem(i + way, 2)
        blk = lax.rem(z + (NZ - step) * dist, NZ)
        view = ring[ch].at[blk, aligned(half, half_rows), :]
        return pltpu.make_async_remote_copy(
            src_ref=view,
            dst_ref=view,
            send_sem=z_send.at[ch, way, i],
            recv_sem=z_recv.at[ch, way, i],
            device_id=device(x, lax.rem(z + step, NZ), c),
            device_id_type=MESH,
        )

    def z_start(ch, i):
        for way in (0, 1):
            hop(ch, way, i).start()

    def z_arrived(ch, i):
        for way in (0, 1):
            hop(ch, way, i).wait_recv()

    def x_copies(ch, peer, slot, mark):
        made = []
        for array, col, w, off in chunks[ch][0]:
            kind = 0 if array == 0 else 1
            made.append(
                pltpu.make_async_remote_copy(
                    src_ref=stage[ch].at[peer, :, off : off + w],
                    dst_ref=outs[array].at[slot, 0:block, col : col + w],
                    send_sem=x_send.at[ch, kind, peer],
                    recv_sem=x_recv.at[ch, kind, mark],
                    device_id=device(peer // NC, z, lax.rem(peer, NC)),
                    device_id_type=MESH,
                )
            )
        return made

    def own_copies(ch):
        return [
            pltpu.make_async_copy(
                stage[ch].at[me, :, off : off + w],
                outs[array].at[me, 0:block, col : col + w],
                own_sem.at[ch, 0 if array == 0 else 1],
            )
            for array, col, w, off in chunks[ch][0]
        ]

    def make_pick():
        earlier = (
            lax.broadcasted_iota(jnp.int32, (tok, tok), 0) < lax.broadcasted_iota(jnp.int32, (tok, tok), 1)
        ).astype(BF16)
        slot_row = lax.broadcasted_iota(jnp.int32, (block, tok), 0).astype(F32)
        peer_row = lax.broadcasted_iota(jnp.int32, (PEERS, tok), 0)
        expert_row = ((peer_row // NC) * (NZ * NC) + z * NC + lax.rem(peer_row, NC)).astype(F32)
        turn = (
            lax.broadcasted_iota(jnp.int32, (LANES, LANES), 0) == lax.broadcasted_iota(jnp.int32, (LANES, LANES), 1)
        ).astype(BF16)

        def one(s, _):
            turned = lax.dot_general(turn, ring[0][s, :, 0:LANES], NT, preferred_element_type=F32)
            match = jnp.zeros((PEERS, tok), F32)
            for k in range(TOP):
                match = match + (jnp.broadcast_to(turned[k : k + 1, :], (PEERS, tok)) == expert_row).astype(F32)
            position = jnp.dot(match.astype(BF16), earlier, preferred_element_type=F32)
            slot = jnp.where(match > 0.0, position + (s * cap).astype(F32), -1.0)
            for peer in range(PEERS):
                hit = jnp.broadcast_to(slot[peer : peer + 1, :], (block, tok)) == slot_row
                pick[peer, :, aligned(s, tok)] = hit.astype(F32).astype(BF16)
            return 0

        lax.fori_loop(0, NZ, one, 0)
        side_out[...] = ring[0][:, :, 0:LANES]

    def pieces(ch, lo, hi):
        def one(peer, _):
            w_all = chunks[ch][1]
            rows = pick[peer]
            for at in range(0, w_all, 256):
                w = min(256, w_all - at)
                cols = ring[ch][:, :, at : at + w].reshape(NZ * tok, w)
                stage[ch][peer, :, at : at + w] = jnp.dot(rows, cols, preferred_element_type=F32).astype(BF16)

            @pl.when(peer != me)
            def _():
                for copy in x_copies(ch, peer, me, me):
                    copy.start()

            @pl.when(peer == me)
            def _():
                for copy in own_copies(ch):
                    copy.start()

            return 0

        lax.fori_loop(lo, hi, one, 0)

    def x_arrived(ch):
        def one(step, _):
            peer = lax.rem(me + step, PEERS)
            for copy in x_copies(ch, peer, peer, peer):
                copy.wait_recv()
            return 0

        lax.fori_loop(1, PEERS, one, 0)
        for copy in own_copies(ch):
            copy.wait()

    per_x = NZ * NC * cap
    new = lax.broadcasted_iota(jnp.int32, (unit, per_x), 0)
    old = lax.broadcasted_iota(jnp.int32, (unit, per_x), 1)
    core = (new >= padded).astype(jnp.int32)
    inner = new - core * padded

    def prepare(b):
        order = jnp.zeros((unit, per_x), jnp.bool_)
        for zed in range(NZ):
            order = order | (
                (inner >= zed * cap) & (inner < (zed + 1) * cap) & (old == inner + zed * (NC - 1) * cap + core * cap)
            )
        moved = jnp.dot(order.astype(F32).astype(BF16), saved[aligned(b, per_x), :], preferred_element_type=F32)
        gate, lift = moved[:, :hidden], moved[:, hidden:]
        sig = jax.nn.sigmoid(gate)
        rows = aligned(b, unit)
        swish = gate * sig
        act[rows, :] = (swish * lift).astype(BF16)
        coef_gate[rows, :] = lift * sig * (1.0 + gate * (1.0 - sig))
        coef_up[rows, :] = swish

    def through_down(b):
        rows = aligned(b, unit)
        two = pl.ds(b * NC, NC)
        dy = dy_rows[two, :, :].reshape(unit, width)
        act_grad = lax.dot_general(dy, down[...].reshape(hidden, width), NT, preferred_element_type=F32)
        gate_grad = jnp.sum(act[rows, :].astype(F32) * act_grad, axis=1, keepdims=True) / jnp.sqrt(F32(width))
        side = side_rows[two, :, :].reshape(unit, LANES).astype(F32)
        mine = expert.astype(F32)
        gain = jnp.zeros((unit, 1), F32)
        for k in range(TOP):
            gain = gain + jnp.where(side[:, k : k + 1] == mine, side[:, GATE_LANE + k : GATE_LANE + k + 1], 0.0)
        lane = lax.broadcasted_iota(jnp.int32, (unit, LANES), 1)
        gate_out[two, :, :] = (
            jnp.where((lane < TOP) & (side == mine), jnp.broadcast_to(gate_grad, (unit, LANES)), 0.0)
            .astype(BF16)
            .reshape(NC, padded, LANES)
        )
        scaled = gain * act_grad
        pre_out[rows, 0:hidden] = (scaled * coef_gate[rows, :]).astype(BF16)
        pre_out[rows, hidden : 2 * hidden] = (scaled * coef_up[rows, :]).astype(BF16)
        for at in range(0, width, 512):
            part = dy_rows[two, :, at : at + 512].reshape(unit, 512).astype(F32)
            dy_rows[two, :, at : at + 512] = (gain * part).astype(BF16).reshape(NC, padded, 512)

    def through_up(b):
        rows = aligned(b, unit)
        two = pl.ds(b * NC, NC)

        def one(q, _):
            grad = lax.dot_general(pre_out[rows, :], up[q], NT, preferred_element_type=F32)
            row_out[two, :, aligned(q, up.shape[1])] = grad.astype(BF16).reshape(NC, padded, up.shape[1])
            return 0

        lax.fori_loop(0, NY, one, 0)

    def down_grad(k):
        cols = aligned(k, 512)
        scaled_dy = dy_rows[:, :, cols].reshape(PEERS * padded, 512)
        dn_out[:, cols] = jnp.dot(turned_act[...], scaled_dy, preferred_element_type=F32).astype(BF16)

    def run(work, lo, hi):
        def one(b, _):
            work(b)
            return 0

        lax.fori_loop(lo, hi, one, 0)

    for k in (0, 1):
        y_own_copy(k).start()
        for h in (0, 2, 1, 3):
            y_copy(k, h).start()
    ticks = sends - 2
    for ch in range(n):
        z_start(ch, 0)
        z_start(ch, 1)
        if ch > 0:
            z_arrived(ch - 1, sends - 2)
            z_arrived(ch - 1, sends - 1)
        if ch == 1:
            make_pick()
        if ch in (1, 2):
            y_forward(ch - 1)

        def tick(i, _, ch=ch):
            z_arrived(ch, i)
            z_start(ch, i + 2)
            if ch == 0:
                run(prepare, (NX * i) // ticks, (NX * (i + 1)) // ticks)
            else:
                pieces(ch - 1, jnp.minimum(3 * i, PEERS), jnp.minimum(3 * i + 3, PEERS))
            return 0

        lax.fori_loop(0, ticks, tick, 0)
        if ch == 0:
            turned_act[...] = act[...].astype(F32).T.astype(BF16)
    z_arrived(n - 1, sends - 2)
    z_arrived(n - 1, sends - 1)
    pieces(n - 1, 0, PEERS)
    for ch in range(n // 2):
        x_arrived(ch)
    y_arrived(0)
    run(through_down, 0, NX)
    y_arrived(1)
    run(through_up, 0, NX)
    run(down_grad, 0, width // 512)
    for ch in range(n):
        if ch >= n // 2:
            x_arrived(ch)

        def drain(i, _, ch=ch):
            for way in (0, 1):
                hop(ch, way, i).wait_send()
            return 0

        lax.fori_loop(0, sends, drain, 0)

        def sent(step, _, ch=ch):
            peer = lax.rem(me + step, PEERS)
            for copy in x_copies(ch, peer, me, me):
                copy.wait_send()
            return 0

        lax.fori_loop(1, PEERS, sent, 0)
    for k in (0, 1):
        for h in range(6):
            y_copy(k, h).wait_send()


def front(side, dy, x, saved, up, down, cap):
    tok, width = dy.shape
    hidden = up.shape[1] // 2
    block = NZ * cap
    padded = -(-block // 16) * 16
    half = width // 2
    chunks = [
        ([(0, 0, LANES, 0), (1, 0, half, LANES)], LANES + half),
        ([(1, half, half, 0)], half),
        ([(2, 0, half, 0)], half),
        ([(2, half, half, 0)], half),
    ]
    n = len(chunks)
    rows = PEERS * padded
    vmem = pl.BlockSpec(memory_space=pltpu.VMEM)
    anywhere = pl.BlockSpec(memory_space=pl.ANY)
    shape = jax.ShapeDtypeStruct
    return pl.pallas_call(
        functools.partial(front_kernel, chunks, cap),
        out_shape=(
            shape((NZ, tok, LANES), BF16),
            shape((PEERS, padded, width), BF16),
            shape((rows, 2 * hidden), BF16),
            shape((PEERS, padded, LANES), BF16),
            shape((PEERS, padded, width), BF16),
            shape((hidden, width), BF16),
        ),
        in_specs=[vmem] * 4 + [anywhere] * 2,
        out_specs=(vmem,) * 6,
        scratch_shapes=[pltpu.VMEM((NZ, tok, w), BF16) for _, w in chunks]
        + [pltpu.VMEM((PEERS, block, w), BF16) for _, w in chunks]
        + [
            pltpu.VMEM((tok, LANES), BF16),
            pltpu.VMEM((PEERS, padded, LANES), BF16),
            pltpu.VMEM((PEERS, padded, width), BF16),
            pltpu.VMEM((PEERS, block, NZ * tok), BF16),
            pltpu.VMEM((NY,) + up.shape, BF16),
            pltpu.VMEM((NY,) + down.shape, BF16),
            pltpu.VMEM((rows, hidden), BF16),
            pltpu.VMEM((hidden, rows), BF16),
            pltpu.VMEM((rows, hidden), F32),
            pltpu.VMEM((rows, hidden), F32),
            pltpu.SemaphoreType.DMA((n, 2, NZ - 1)),
            pltpu.SemaphoreType.DMA((n, 2, NZ - 1)),
            pltpu.SemaphoreType.DMA((n, 2, PEERS)),
            pltpu.SemaphoreType.DMA((n, 2, PEERS)),
            pltpu.SemaphoreType.DMA((n, 2)),
            pltpu.SemaphoreType.DMA((2, 6)),
            pltpu.SemaphoreType.DMA((2, 6)),
            pltpu.SemaphoreType.DMA((2,)),
        ],
        compiler_params=pltpu.CompilerParams(collective_id=0, has_side_effects=True, vmem_limit_bytes=62 << 20),
        cost_estimate=pl.CostEstimate(flops=20_000_000_000, bytes_accessed=350_000_000, transcendentals=0),
        name="front",
    )(side, dy, x, saved, up, down)


def back_kernel(
    chunks, cap, scale, side_ref, gate_ref, row_ref, x_ref, pre_ref, gate_out, tok_out, gu_out, *scratch
):
    n = len(chunks)
    landed, total, leave, come = (scratch[k * n : (k + 1) * n] for k in range(4))
    spread, gu_leave, gu_come, z_send, z_recv, x_send, x_recv, own_sem, y_send, y_recv = scratch[4 * n :]
    ins, outs = (gate_ref, row_ref), (gate_out, tok_out)
    x, z, c = place()
    y = lax.axis_index("dp")
    me = x * NC + c
    tok = tok_out.shape[0]
    half_rows = tok // 2
    block = NZ * cap
    padded = row_ref.shape[1]
    pad = landed[0].shape[1]
    sends = NZ - 1

    for buf, (_, w) in zip(landed, chunks):
        buf[:, block:, :] = jnp.zeros((PEERS, pad - block, w), BF16)
    enter(x, z, c)

    def x_copies(ch, src_slot, dst_slot, mark, peer):
        made = []
        for array, col, w, off in chunks[ch][0]:
            made.append(
                pltpu.make_async_remote_copy(
                    src_ref=ins[array].at[src_slot, 0:block, col : col + w],
                    dst_ref=landed[ch].at[dst_slot, 0:block, off : off + w],
                    send_sem=x_send.at[ch, array, peer],
                    recv_sem=x_recv.at[ch, array, mark],
                    device_id=device(peer // NC, z, lax.rem(peer, NC)),
                    device_id_type=MESH,
                )
            )
        return made

    def own_copies(ch):
        return [
            pltpu.make_async_copy(
                ins[array].at[me, 0:block, col : col + w], landed[ch].at[me, 0:block, off : off + w], own_sem.at[ch, array]
            )
            for array, col, w, off in chunks[ch][0]
        ]

    for ch in range(n):

        def send(step, _, ch=ch):
            peer = lax.rem(me + step, PEERS)
            for copy in x_copies(ch, peer, me, me, peer):
                copy.start()
            return 0

        lax.fori_loop(1, PEERS, send, 0)
        for copy in own_copies(ch):
            copy.start()

    gu_rows = gu_out.shape[0]
    half_gu = gu_rows // 2

    def gu_part(ahead, half):
        first = lax.rem(y + ahead, NY) * gu_rows + half * half_gu
        cols = x_ref[:, :, pl.ds(pl.multiple_of(first, half_gu), half_gu)].reshape(PEERS * padded, half_gu)
        return lax.dot_general(cols, pre_ref[...], TN, preferred_element_type=F32)

    def gu_hop(k):
        return pltpu.make_async_remote_copy(
            src_ref=gu_leave.at[k],
            dst_ref=gu_come.at[k],
            send_sem=y_send.at[k],
            recv_sem=y_recv.at[k],
            device_id=along_y(1 if k < 3 else NY - 1),
            device_id_type=MESH,
        )

    def gu_send(k):
        up = k < 3
        ahead = 2 if k in (0, 3) else (1 if up else NY - 1)
        half = (0 if up else 1) if k in (0, 2, 3, 5) else (1 if up else 0)
        value = gu_part(ahead, half)
        if k in (2, 5):
            gu_hop(k - 2).wait_recv()
            value = value + gu_come[k - 2].astype(F32)
        gu_leave[k] = value.astype(BF16)
        gu_hop(k).start()

    def gu_own(half):
        gu_out[half * half_gu : (half + 1) * half_gu, :] = gu_part(0, half)

    def gu_finish():
        for half in (0, 1):
            rows = slice(half * half_gu, (half + 1) * half_gu)
            a, b = (2, 4) if half == 0 else (1, 5)
            gu_hop(a).wait_recv()
            gu_hop(b).wait_recv()
            gu_out[rows, :] = (gu_out[rows, :] + gu_come[a].astype(F32) + gu_come[b].astype(F32)) * scale

    gu_send(0)
    gu_send(3)

    later = (
        lax.broadcasted_iota(jnp.int32, (tok, tok), 1) < lax.broadcasted_iota(jnp.int32, (tok, tok), 0)
    ).astype(BF16)
    lane = lax.broadcasted_iota(jnp.int32, (tok, LANES), 1)
    expert_lane = jnp.where(lane < PEERS, (lane // NC) * (NZ * NC) + z * NC + lax.rem(lane, NC), -1).astype(F32)
    slot_lane = lax.broadcasted_iota(jnp.int32, (tok, pad), 1).astype(F32)

    def spread_one(s, _):
        side = side_ref[s].astype(F32)
        match = jnp.zeros((tok, LANES), F32)
        for k in range(TOP):
            match = match + (jnp.broadcast_to(side[:, k : k + 1], (tok, LANES)) == expert_lane).astype(F32)
        position = jnp.dot(later, match.astype(BF16), preferred_element_type=F32)
        slot = jnp.where(match > 0.0, position + (s * cap).astype(F32), -1.0)
        for peer in range(PEERS):
            hit = jnp.broadcast_to(slot[:, peer : peer + 1], (tok, pad)) == slot_lane
            spread[s, :, peer * pad : (peer + 1) * pad] = hit.astype(F32).astype(BF16)
        return 0

    lax.fori_loop(0, NZ, spread_one, 0)

    def x_arrived(ch):
        def one(step, _):
            peer = lax.rem(me + step, PEERS)
            for copy in x_copies(ch, peer, peer, peer, peer):
                copy.wait_recv()
            return 0

        lax.fori_loop(1, PEERS, one, 0)
        for copy in own_copies(ch):
            copy.wait()

    def combines(ch, lo, hi):
        def one(k, _):
            width = chunks[ch][1]
            s = lax.rem(z + NZ // 2 + k, NZ)
            rows = spread[s]
            for at in range(0, width, 256):
                w = min(256, width - at)
                cols = landed[ch][:, :, at : at + w].reshape(PEERS * pad, w)
                total[ch][s, :, at : at + w] = jnp.dot(rows, cols, preferred_element_type=F32)
            return 0

        lax.fori_loop(lo, hi, one, 0)

    def hop(ch, way, i):
        step = 1 if way == 0 else NZ - 1
        return pltpu.make_async_remote_copy(
            src_ref=leave[ch].at[way, i],
            dst_ref=come[ch].at[way, i],
            send_sem=z_send.at[ch, way, i],
            recv_sem=z_recv.at[ch, way, i],
            device_id=device(x, lax.rem(z + step, NZ), c),
            device_id_type=MESH,
        )

    def z_step(ch, i, first):
        for way in (0, 1):
            step = 1 if way == 0 else NZ - 1
            dist = NZ // 2 - (i + 1) // 2
            half = lax.rem(i + way, 2)
            s = lax.rem(z + step * dist, NZ)
            value = total[ch][s, aligned(half, half_rows), :]
            if not first:
                hop(ch, way, i - 2).wait_recv()
                value = value + come[ch][way, i - 2].astype(F32)
            leave[ch][way, i] = value.astype(BF16)
            hop(ch, way, i).start()

    def finish(ch):
        for way in (0, 1):
            hop(ch, way, sends - 2).wait_recv()
            hop(ch, way, sends - 1).wait_recv()
        for half in (0, 1):
            rows = slice(half * half_rows, (half + 1) * half_rows)
            value = total[ch][z, rows, :]
            for way in (0, 1):
                i = sends - 1 if (sends - 1 + way) % 2 == half else sends - 2
                value = value + come[ch][way, i].astype(F32)
            for array, col, w, off in chunks[ch][0]:
                outs[array][rows, col : col + w] = value[:, off : off + w].astype(BF16)

    x_arrived(0)
    combines(0, 0, NZ)
    ticks = sends - 2
    extra = {0: (lambda: gu_send(1), lambda: gu_send(4)), 1: (lambda: gu_send(2), lambda: gu_send(5)), 2: (lambda: gu_own(0), lambda: gu_own(1))}
    for ch in range(n):
        z_step(ch, 0, True)
        z_step(ch, 1, True)
        if ch > 0:
            finish(ch - 1)
        for work in extra.get(ch, ()):
            work()
        if ch + 1 < n:
            x_arrived(ch + 1)

        def tick(i, _, ch=ch):
            z_step(ch, i + 2, False)
            if ch + 1 < n:
                combines(ch + 1, (NZ * i) // ticks, (NZ * (i + 1)) // ticks)
            return 0

        lax.fori_loop(0, ticks, tick, 0)
    finish(n - 1)
    gu_finish()
    for ch in range(n):

        def drain(i, _, ch=ch):
            for way in (0, 1):
                hop(ch, way, i).wait_send()
            return 0

        lax.fori_loop(0, sends, drain, 0)

        def sent(step, _, ch=ch):
            peer = lax.rem(me + step, PEERS)
            for copy in x_copies(ch, peer, me, me, peer):
                copy.wait_send()
            return 0

        lax.fori_loop(1, PEERS, sent, 0)
    for k in range(6):
        gu_hop(k).wait_send()


def back(side, gate_rows, rows, x_rows, pre, cap, gu_rows, scale):
    width = rows.shape[2]
    tok = side.shape[1]
    pad = -(-NZ * cap // LANES) * LANES
    quarter = width // 4
    chunks = [([(0, 0, LANES, 0), (1, 0, quarter, LANES)], LANES + quarter)]
    chunks += [([(1, k * quarter, quarter, 0)], quarter) for k in (1, 2, 3)]
    n = len(chunks)
    vmem = pl.BlockSpec(memory_space=pltpu.VMEM)
    shape = jax.ShapeDtypeStruct
    return pl.pallas_call(
        functools.partial(back_kernel, chunks, cap, scale),
        out_shape=(shape((tok, LANES), BF16), shape((tok, width), BF16), shape((gu_rows, pre.shape[1]), F32)),
        in_specs=[vmem] * 5,
        out_specs=(vmem,) * 3,
        scratch_shapes=[pltpu.VMEM((PEERS, pad, w), BF16) for _, w in chunks]
        + [pltpu.VMEM((NZ, tok, w), F32) for _, w in chunks]
        + [pltpu.VMEM((2, NZ - 1, tok // 2, w), BF16) for _, w in chunks] * 2
        + [
            pltpu.VMEM((NZ, tok, PEERS * pad), BF16),
            pltpu.VMEM((6, gu_rows // 2, pre.shape[1]), BF16),
            pltpu.VMEM((6, gu_rows // 2, pre.shape[1]), BF16),
            pltpu.SemaphoreType.DMA((n, 2, NZ - 1)),
            pltpu.SemaphoreType.DMA((n, 2, NZ - 1)),
            pltpu.SemaphoreType.DMA((n, 2, PEERS)),
            pltpu.SemaphoreType.DMA((n, 2, PEERS)),
            pltpu.SemaphoreType.DMA((n, 2)),
            pltpu.SemaphoreType.DMA((6,)),
            pltpu.SemaphoreType.DMA((6,)),
        ],
        compiler_params=pltpu.CompilerParams(collective_id=1, has_side_effects=True, vmem_limit_bytes=62 << 20),
        cost_estimate=pl.CostEstimate(flops=10_000_000_000, bytes_accessed=250_000_000, transcendentals=0),
        name="back",
    )(side, gate_rows, rows, x_rows, pre)


def on_device(tokens, out_grad, routes, gate_weights, saved_preacts, gate_up, down_proj):
    groups = lax.axis_size("dp")
    tok_rows, top = routes.shape
    cap = saved_preacts.shape[2] // lax.axis_size("expert")
    zeros = functools.partial(jnp.zeros, dtype=BF16)
    side = jnp.concatenate(
        [
            routes.T.astype(BF16),
            zeros((GATE_LANE - top, tok_rows)),
            gate_weights.T,
            zeros((LANES - GATE_LANE - top, tok_rows)),
        ]
    )
    sides, x_rows, pre, gate_rows, rows, grad_dn = front(
        side, out_grad, tokens, saved_preacts[0, 0], gate_up[0], down_proj[0], cap
    )
    grad_scale = float(1.0 / (groups * tok_rows * top) ** 0.5)
    grad_dn = lax.psum_scatter(grad_dn, "dp", scatter_dimension=0, tiled=True).astype(F32) * grad_scale
    gates, grad_tokens, grad_gu = back(sides, gate_rows, rows, x_rows, pre, cap, gate_up.shape[1], grad_scale)
    return (grad_tokens, gates[:, :top], grad_gu[None], grad_dn[None])


def solution(mesh):
    in_specs = (
        P(("dp", "expert"), None),
        P(("dp", "expert"), None),
        P(("dp", "expert"), None),
        P(("dp", "expert"), None),
        P("dp", "expert", None, None),
        P("expert", "dp", None),
        P("expert", "dp", None),
    )
    out_specs = (
        P(("dp", "expert"), None),
        P(("dp", "expert"), None),
        P("expert", "dp", None),
        P("expert", "dp", None),
    )
    return jax.shard_map(
        on_device, mesh=mesh, in_specs=in_specs, out_specs=out_specs, check_vma=False
    )
```

```python
import functools

import jax
import jax.numpy as jnp
from jax import lax
from jax.experimental import pallas as pl
from jax.experimental.pallas import tpu as pltpu
from jax.sharding import PartitionSpec as P

MESH = pl.DeviceIdType.MESH
BF16, F32 = jnp.bfloat16, jnp.float32
NX, NZ, NC = 4, 8, 2
NY = 4
PEERS = NX * NC
LANES = 128
TOP = 6
DY_CHUNKS, X_CHUNKS = (512, 768, 768), (768, 768, 512)
BACK_CHUNKS = (256, 384, 512, 512, 384)
GATE_LANE = 8
NT = (((1,), (1,)), ((), ()))
TN = (((0,), (0,)), ((), ()))


def place():
    e = lax.axis_index("expert")
    return e // (NZ * NC), lax.rem(e // NC, NZ), lax.rem(e, NC)


def device(x, z, c):
    return (lax.axis_index("dp"), (x * NZ + z) * NC + c)


def along_y(step):
    return (lax.rem(lax.axis_index("dp") + step, NY), lax.axis_index("expert"))


def enter(x, z, c):
    barrier = pltpu.get_barrier_semaphore()
    for step in (1, NZ - 1):
        pl.semaphore_signal(barrier, inc=1, device_id=device(x, lax.rem(z + step, NZ), c), device_id_type=MESH)
    for step in (1, NY - 1):
        pl.semaphore_signal(barrier, inc=1, device_id=along_y(step), device_id_type=MESH)
    me = x * NC + c
    for step in range(1, PEERS):
        peer = lax.rem(me + step, PEERS)
        pl.semaphore_signal(barrier, inc=1, device_id=device(peer // NC, z, lax.rem(peer, NC)), device_id_type=MESH)
    pl.semaphore_wait(barrier, 2 + 2 + PEERS - 1)


def aligned(index, size):
    return pl.ds(pl.multiple_of(index * size, size), size)


def front_kernel(
    chunks,
    cap,
    scale,
    side_in,
    dy_in,
    x_in,
    saved,
    up_in,
    down_in,
    side_out,
    x_out,
    pre_out,
    gate_out,
    row_out,
    dn_out,
    *scratch,
):
    n = len(chunks)
    ring, stage = scratch[:n], scratch[n : n + n // 2] * 2
    later = scratch[n + n // 2 :]
    side_own, side_rows, dy_rows, scaled_rows, pick, up, down, act, turned_act, coef_gate, coef_up, dn, dn_come, dn_sum = later[:14]
    z_send, z_recv, x_send, x_recv, own_sem, y_send, y_recv, y_own, d_send, d_recv = later[14:]
    ins, outs = (side_own, dy_in, x_in), (side_rows, dy_rows, x_out)
    x, z, c = place()
    y = lax.axis_index("dp")
    expert = lax.axis_index("expert")
    me = x * NC + c
    tok, width = dy_in.shape
    half_rows = tok // 2
    block = pick.shape[1]
    padded = dy_rows.shape[1]
    hidden = act.shape[1]
    sends = NZ - 1
    unit = NC * padded

    eye = (lax.broadcasted_iota(jnp.int32, (tok, tok), 0) == lax.broadcasted_iota(jnp.int32, (tok, tok), 1)).astype(BF16)
    side_own[...] = lax.dot_general(eye, side_in[...], NT, preferred_element_type=F32).astype(BF16)
    for segments, buf in ((s, b) for (s, _), b in zip(chunks, ring)):
        for array, col, w, off in segments:
            buf[z, :, off : off + w] = ins[array][:, col : col + w]
    for buf in outs:
        buf[:, block:, :] = jnp.zeros((PEERS, padded - block, buf.shape[2]), BF16)
    enter(x, z, c)

    weights = ((down_in, down), (up_in, up))

    def y_copy(k, hop):
        source, whole = weights[k]
        rows = whole.shape[1]
        cut = rows // 32 * 16
        first, second = (0, cut), (cut, rows - cut)
        lo, size = (first, second, second, first, first, second)[hop]
        step = 1 if hop in (0, 1, 4) else NY - 1
        back = NY - step
        slot = y if hop < 4 else lax.rem(y + back, NY)
        src = source.at[lo : lo + size, :] if hop < 4 else whole.at[slot, lo : lo + size, :]
        return pltpu.make_async_remote_copy(
            src_ref=src,
            dst_ref=whole.at[slot, lo : lo + size, :],
            send_sem=y_send.at[k, hop],
            recv_sem=y_recv.at[k, hop],
            device_id=along_y(step),
            device_id_type=MESH,
        )

    def y_own_copy(k):
        return pltpu.make_async_copy(weights[k][0], weights[k][1].at[y], y_own.at[k])

    def y_forward(k):
        y_copy(k, 0).wait_recv()
        y_copy(k, 4).start()
        y_copy(k, 2).wait_recv()
        y_copy(k, 5).start()

    def y_arrived(k):
        for hop in (1, 3, 4, 5):
            y_copy(k, hop).wait_recv()
        y_own_copy(k).wait()

    def hop(ch, way, i):
        step = 1 if way == 0 else NZ - 1
        dist = i // 2
        half = lax.rem(i + way, 2)
        blk = lax.rem(z + (NZ - step) * dist, NZ)
        view = ring[ch].at[blk, aligned(half, half_rows), :]
        return pltpu.make_async_remote_copy(
            src_ref=view,
            dst_ref=view,
            send_sem=z_send.at[ch, way, i],
            recv_sem=z_recv.at[ch, way, i],
            device_id=device(x, lax.rem(z + step, NZ), c),
            device_id_type=MESH,
        )

    def z_start(ch, i):
        for way in (0, 1):
            hop(ch, way, i).start()

    def z_arrived(ch, i):
        for way in (0, 1):
            hop(ch, way, i).wait_recv()

    def x_copies(ch, peer, slot, mark):
        made = []
        for array, col, w, off in chunks[ch][0]:
            kind = 0 if array == 0 else 1
            made.append(
                pltpu.make_async_remote_copy(
                    src_ref=stage[ch].at[peer, :, off : off + w],
                    dst_ref=outs[array].at[slot, 0:block, col : col + w],
                    send_sem=x_send.at[ch, kind, peer],
                    recv_sem=x_recv.at[ch, kind, mark],
                    device_id=device(peer // NC, z, lax.rem(peer, NC)),
                    device_id_type=MESH,
                )
            )
        return made

    def own_copies(ch):
        return [
            pltpu.make_async_copy(
                stage[ch].at[me, :, off : off + w],
                outs[array].at[me, 0:block, col : col + w],
                own_sem.at[ch, 0 if array == 0 else 1],
            )
            for array, col, w, off in chunks[ch][0]
        ]

    def make_pick():
        earlier = (
            lax.broadcasted_iota(jnp.int32, (tok, tok), 0) < lax.broadcasted_iota(jnp.int32, (tok, tok), 1)
        ).astype(BF16)
        slot_row = lax.broadcasted_iota(jnp.int32, (block, tok), 0).astype(F32)
        peer_row = lax.broadcasted_iota(jnp.int32, (PEERS, tok), 0)
        expert_row = ((peer_row // NC) * (NZ * NC) + z * NC + lax.rem(peer_row, NC)).astype(F32)
        turn = (
            lax.broadcasted_iota(jnp.int32, (LANES, LANES), 0) == lax.broadcasted_iota(jnp.int32, (LANES, LANES), 1)
        ).astype(BF16)

        def one(s, _):
            turned = lax.dot_general(turn, ring[0][s, :, 0:LANES], NT, preferred_element_type=F32)
            match = jnp.zeros((PEERS, tok), F32)
            for k in range(TOP):
                match = match + (jnp.broadcast_to(turned[k : k + 1, :], (PEERS, tok)) == expert_row).astype(F32)
            position = jnp.dot(match.astype(BF16), earlier, preferred_element_type=F32)
            slot = jnp.where(match > 0.0, position + (s * cap).astype(F32), -1.0)
            for peer in range(PEERS):
                hit = jnp.broadcast_to(slot[peer : peer + 1, :], (block, tok)) == slot_row
                pick[peer, :, aligned(s, tok)] = hit.astype(F32).astype(BF16)
            return 0

        lax.fori_loop(0, NZ, one, 0)
        side_out[...] = ring[0][:, :, 0:LANES]

    def pieces(ch, lo, hi):
        def one(peer, _):
            w_all = chunks[ch][1]
            rows = pick[peer]
            for at in range(0, w_all, 256):
                w = min(256, w_all - at)
                cols = ring[ch][:, :, at : at + w].reshape(NZ * tok, w)
                stage[ch][peer, :, at : at + w] = jnp.dot(rows, cols, preferred_element_type=F32).astype(BF16)

            @pl.when(peer != me)
            def _():
                for copy in x_copies(ch, peer, me, me):
                    copy.start()

            @pl.when(peer == me)
            def _():
                for copy in own_copies(ch):
                    copy.start()

            return 0

        lax.fori_loop(lo, hi, one, 0)

    per_x = NZ * NC * cap
    new = lax.broadcasted_iota(jnp.int32, (unit, per_x), 0)
    old = lax.broadcasted_iota(jnp.int32, (unit, per_x), 1)
    core = (new >= padded).astype(jnp.int32)
    inner = new - core * padded

    def prepare(b):
        order = jnp.zeros((unit, per_x), jnp.bool_)
        for zed in range(NZ):
            order = order | (
                (inner >= zed * cap) & (inner < (zed + 1) * cap) & (old == inner + zed * (NC - 1) * cap + core * cap)
            )
        moved = jnp.dot(order.astype(F32).astype(BF16), saved[aligned(b, per_x), :], preferred_element_type=F32)
        gate, lift = moved[:, :hidden], moved[:, hidden:]
        sig = jax.nn.sigmoid(gate)
        rows = aligned(b, unit)
        swish = gate * sig
        act[rows, :] = (swish * lift).astype(BF16)
        coef_gate[rows, :] = lift * sig * (1.0 + gate * (1.0 - sig))
        coef_up[rows, :] = swish

    def gain_of(b):
        side = side_rows[pl.ds(b * NC, NC), :, :].reshape(unit, LANES).astype(F32)
        mine = expert.astype(F32)
        gain = jnp.zeros((unit, 1), F32)
        for k in range(TOP):
            gain = gain + jnp.where(side[:, k : k + 1] == mine, side[:, GATE_LANE + k : GATE_LANE + k + 1], 0.0)
        return side, mine, gain

    def scale_rows(b):
        two = pl.ds(b * NC, NC)
        gain = gain_of(b)[2]
        for at in range(0, width, 512):
            part = dy_rows[two, :, at : at + 512].reshape(unit, 512).astype(F32)
            scaled_rows[two, :, at : at + 512] = (gain * part).astype(BF16).reshape(NC, padded, 512)

    def through_down(b):
        rows = aligned(b, unit)
        two = pl.ds(b * NC, NC)
        dy = dy_rows[two, :, :].reshape(unit, width)
        act_grad = lax.dot_general(dy, down[...].reshape(hidden, width), NT, preferred_element_type=F32)
        gate_grad = jnp.sum(act[rows, :].astype(F32) * act_grad, axis=1, keepdims=True) / jnp.sqrt(F32(width))
        side, mine, gain = gain_of(b)
        lane = lax.broadcasted_iota(jnp.int32, (unit, LANES), 1)
        gate_out[two, :, :] = (
            jnp.where((lane < TOP) & (side == mine), jnp.broadcast_to(gate_grad, (unit, LANES)), 0.0)
            .astype(BF16)
            .reshape(NC, padded, LANES)
        )
        scaled = gain * act_grad
        pre_out[rows, 0:hidden] = (scaled * coef_gate[rows, :]).astype(BF16)
        pre_out[rows, hidden : 2 * hidden] = (scaled * coef_up[rows, :]).astype(BF16)

    def through_up(b):
        rows = aligned(b, unit)
        two = pl.ds(b * NC, NC)

        def one(q, _):
            grad = lax.dot_general(pre_out[rows, :], up[q], NT, preferred_element_type=F32)
            row_out[two, :, aligned(q, up.shape[1])] = grad.astype(BF16).reshape(NC, padded, up.shape[1])
            return 0

        lax.fori_loop(0, NY, one, 0)

    def down_grad(k):
        cols = aligned(k, 512)
        scaled_dy = scaled_rows[:, :, cols].reshape(PEERS * padded, 512)
        dn[:, :, cols] = (
            jnp.dot(turned_act[...], scaled_dy, preferred_element_type=F32).astype(BF16).reshape(NY, hidden // NY, 512)
        )

    dn_rows = hidden // NY
    dn_cut = dn_rows // 32 * 16
    spans = ((0, dn_cut), (dn_cut, dn_rows - dn_cut))

    def dn_hop(k):
        lo, size = spans[(0, 1, 0, 1, 0, 1)[k]]
        src = dn_sum.at[k // 3, 0:size, :]
        if k in (0, 1, 3, 4):
            ahead = (2, 1, 0, 2, NY - 1)[k]
            src = dn.at[lax.rem(y + ahead, NY), lo : lo + size, :]
        return pltpu.make_async_remote_copy(
            src_ref=src,
            dst_ref=dn_come.at[k, 0:size, :],
            send_sem=d_send.at[k],
            recv_sem=d_recv.at[k],
            device_id=along_y(1 if k < 3 else NY - 1),
            device_id_type=MESH,
        )

    def dn_pass_on():
        for k in (2, 5):
            lo, size = spans[0 if k == 2 else 1]
            dn_hop(k - 2).wait_recv()
            own = dn[lax.rem(y + (1 if k == 2 else NY - 1), NY), lo : lo + size, :].astype(F32)
            dn_sum[k // 3, 0:size, :] = (own + dn_come[k - 2, 0:size, :].astype(F32)).astype(BF16)
            dn_hop(k).start()

    def dn_finish():
        for (lo, size), (a, b) in zip(spans, ((2, 4), (1, 5))):
            dn_hop(a).wait_recv()
            dn_hop(b).wait_recv()
            value = dn[y, lo : lo + size, :].astype(F32)
            value = value + dn_come[a, 0:size, :].astype(F32) + dn_come[b, 0:size, :].astype(F32)
            dn_out[lo : lo + size, :] = value * scale

    def run(work, lo, hi):
        def one(b, _):
            work(b)
            return 0

        lax.fori_loop(lo, hi, one, 0)

    for k in (0, 1):
        y_own_copy(k).start()
        for h in (0, 2, 1, 3):
            y_copy(k, h).start()
    ticks = sends - 2
    half_n = n // 2

    def drained(ch):
        def sent(step, _):
            peer = lax.rem(me + step, PEERS)
            for copy in x_copies(ch, peer, me, me):
                copy.wait_send()
            return 0

        lax.fori_loop(1, PEERS, sent, 0)

    def own_landed(ch):
        for copy in own_copies(ch):
            copy.wait()

    def free_stage(ch):
        if ch >= half_n:
            drained(ch - half_n)

    def x_landed(ch):
        def one(step, _):
            peer = lax.rem(me + step, PEERS)
            for copy in x_copies(ch, peer, peer, peer):
                copy.wait_recv()
            return 0

        lax.fori_loop(1, PEERS, one, 0)

    z_start(0, 0)
    z_start(0, 1)
    for ch in range(n):
        if ch > 0:
            z_arrived(ch - 1, sends - 2)
            z_arrived(ch - 1, sends - 1)
            free_stage(ch - 1)
        if ch > 1:
            own_landed(ch - 2)
        if ch == 1:
            make_pick()
        if ch in (2, 3):
            y_forward(ch - 2)

        def tick(i, _, ch=ch):
            z_arrived(ch, i)
            z_start(ch, i + 2)
            if ch + 1 < n:

                @pl.when(i >= ticks - 2)
                def _():
                    z_start(ch + 1, i - (ticks - 2))

            if ch == 0:
                run(prepare, (NX * i) // ticks, (NX * (i + 1)) // ticks)
            else:
                pieces(ch - 1, jnp.minimum(4 * i, PEERS), jnp.minimum(4 * i + 4, PEERS))
            if ch == half_n + 1:

                @pl.when(i == 2)
                def _():
                    for k in range(half_n):
                        x_landed(k)
                    run(scale_rows, 0, NX)

                tiles = width // 512
                run(down_grad, jnp.clip(2 * (i - 3), 0, tiles), jnp.clip(2 * (i - 2), 0, tiles))
            if ch == n - 1:

                @pl.when(i == 0)
                def _():
                    y_arrived(0)

                run(through_down, jnp.maximum(i - 1, 0), i)
            return 0

        lax.fori_loop(0, ticks, tick, 0)
        if ch == 0:
            turned_act[...] = act[...].astype(F32).T.astype(BF16)
        if ch == half_n + 1:
            for k in (0, 3, 1, 4):
                dn_hop(k).start()
    z_arrived(n - 1, sends - 2)
    z_arrived(n - 1, sends - 1)
    free_stage(n - 1)
    pieces(n - 1, 0, PEERS)
    dn_pass_on()
    y_arrived(1)
    run(through_up, 0, NX)
    dn_finish()
    for ch in range(n):
        if ch >= half_n:
            x_landed(ch)
            drained(ch)
        if ch >= n - 2:
            own_landed(ch)

        def drain(i, _, ch=ch):
            for way in (0, 1):
                hop(ch, way, i).wait_send()
            return 0

        lax.fori_loop(0, sends, drain, 0)
    for k in (0, 1):
        for h in range(6):
            y_copy(k, h).wait_send()
    for k in range(6):
        dn_hop(k).wait_send()


def front(side, dy, x, saved, up, down, cap, scale):
    tok, width = dy.shape
    hidden = up.shape[1] // 2
    block = NZ * cap
    padded = -(-block // 16) * 16
    chunks = []
    for array, widths in ((1, DY_CHUNKS), (2, X_CHUNKS)):
        col = 0
        for w in widths:
            off = 0 if chunks else LANES
            chunks.append(([(0, 0, LANES, 0)] * (off > 0) + [(array, col, w, off)], off + w))
            col += w
    n = len(chunks)
    rows = PEERS * padded
    dn_part = hidden // NY - hidden // NY // 32 * 16
    vmem = pl.BlockSpec(memory_space=pltpu.VMEM)
    anywhere = pl.BlockSpec(memory_space=pl.ANY)
    shape = jax.ShapeDtypeStruct
    return pl.pallas_call(
        functools.partial(front_kernel, chunks, cap, scale),
        out_shape=(
            shape((NZ, tok, LANES), BF16),
            shape((PEERS, padded, width), BF16),
            shape((rows, 2 * hidden), BF16),
            shape((PEERS, padded, LANES), BF16),
            shape((PEERS, padded, width), BF16),
            shape((hidden // NY, width), F32),
        ),
        in_specs=[vmem] * 4 + [anywhere] * 2,
        out_specs=(vmem,) * 6,
        scratch_shapes=[pltpu.VMEM((NZ, tok, w), BF16) for _, w in chunks]
        + [pltpu.VMEM((PEERS, block, max(a[1], b[1])), BF16) for a, b in zip(chunks[: n // 2], chunks[n // 2 :])]
        + [
            pltpu.VMEM((tok, LANES), BF16),
            pltpu.VMEM((PEERS, padded, LANES), BF16),
            pltpu.VMEM((PEERS, padded, width), BF16),
            pltpu.VMEM((PEERS, padded, width), BF16),
            pltpu.VMEM((PEERS, block, NZ * tok), BF16),
            pltpu.VMEM((NY,) + up.shape, BF16),
            pltpu.VMEM((NY,) + down.shape, BF16),
            pltpu.VMEM((rows, hidden), BF16),
            pltpu.VMEM((hidden, rows), BF16),
            pltpu.VMEM((rows, hidden), F32),
            pltpu.VMEM((rows, hidden), F32),
            pltpu.VMEM((NY, hidden // NY, width), BF16),
            pltpu.VMEM((6, dn_part, width), BF16),
            pltpu.VMEM((2, dn_part, width), BF16),
            pltpu.SemaphoreType.DMA((n, 2, NZ - 1)),
            pltpu.SemaphoreType.DMA((n, 2, NZ - 1)),
            pltpu.SemaphoreType.DMA((n, 2, PEERS)),
            pltpu.SemaphoreType.DMA((n, 2, PEERS)),
            pltpu.SemaphoreType.DMA((n, 2)),
            pltpu.SemaphoreType.DMA((2, 6)),
            pltpu.SemaphoreType.DMA((2, 6)),
            pltpu.SemaphoreType.DMA((2,)),
            pltpu.SemaphoreType.DMA((6,)),
            pltpu.SemaphoreType.DMA((6,)),
        ],
        compiler_params=pltpu.CompilerParams(collective_id=0, has_side_effects=True, vmem_limit_bytes=62 << 20),
        cost_estimate=pl.CostEstimate(flops=20_000_000_000, bytes_accessed=350_000_000, transcendentals=0),
        name="front",
    )(side, dy, x, saved, up, down)


def back_kernel(
    chunks, cap, scale, side_ref, gate_ref, row_ref, x_ref, pre_ref, gate_out, tok_out, gu_out, *scratch
):
    n = len(chunks)
    landed, total, leave, come = (scratch[k * n : (k + 1) * n] for k in range(4))
    spread, gu_leave, gu_come, z_send, z_recv, x_send, x_recv, own_sem, y_send, y_recv = scratch[4 * n :]
    ins, outs = (gate_ref, row_ref), (gate_out, tok_out)
    x, z, c = place()
    y = lax.axis_index("dp")
    me = x * NC + c
    tok = tok_out.shape[0]
    half_rows = tok // 2
    block = NZ * cap
    padded = row_ref.shape[1]
    pad = landed[0].shape[1]
    sends = NZ - 1

    for buf, (_, w) in zip(landed, chunks):
        buf[:, block:, :] = jnp.zeros((PEERS, pad - block, w), BF16)
    enter(x, z, c)

    def x_copies(ch, src_slot, dst_slot, mark, peer):
        made = []
        for array, col, w, off in chunks[ch][0]:
            made.append(
                pltpu.make_async_remote_copy(
                    src_ref=ins[array].at[src_slot, 0:block, col : col + w],
                    dst_ref=landed[ch].at[dst_slot, 0:block, off : off + w],
                    send_sem=x_send.at[ch, array, peer],
                    recv_sem=x_recv.at[ch, array, mark],
                    device_id=device(peer // NC, z, lax.rem(peer, NC)),
                    device_id_type=MESH,
                )
            )
        return made

    def own_copies(ch):
        return [
            pltpu.make_async_copy(
                ins[array].at[me, 0:block, col : col + w], landed[ch].at[me, 0:block, off : off + w], own_sem.at[ch, array]
            )
            for array, col, w, off in chunks[ch][0]
        ]

    def x_start(ch):
        def send(step, _):
            peer = lax.rem(me + step, PEERS)
            for copy in x_copies(ch, peer, me, me, peer):
                copy.start()
            return 0

        lax.fori_loop(1, PEERS, send, 0)
        for copy in own_copies(ch):
            copy.start()

    x_start(0)
    x_start(1)

    gu_rows = gu_out.shape[0]
    half_gu = gu_rows // 2

    def gu_part(ahead, half):
        first = lax.rem(y + ahead, NY) * gu_rows + half * half_gu
        cols = x_ref[:, :, pl.ds(pl.multiple_of(first, half_gu), half_gu)].reshape(PEERS * padded, half_gu)
        return lax.dot_general(cols, pre_ref[...], TN, preferred_element_type=F32)

    def gu_hop(k):
        return pltpu.make_async_remote_copy(
            src_ref=gu_leave.at[k],
            dst_ref=gu_come.at[k],
            send_sem=y_send.at[k],
            recv_sem=y_recv.at[k],
            device_id=along_y(1 if k < 3 else NY - 1),
            device_id_type=MESH,
        )

    def gu_send(k):
        up = k < 3
        ahead = 2 if k in (0, 3) else (1 if up else NY - 1)
        half = (0 if up else 1) if k in (0, 2, 3, 5) else (1 if up else 0)
        value = gu_part(ahead, half)
        if k in (2, 5):
            gu_hop(k - 2).wait_recv()
            value = value + gu_come[k - 2].astype(F32)
        gu_leave[k] = value.astype(BF16)
        gu_hop(k).start()

    def gu_own(half):
        gu_out[half * half_gu : (half + 1) * half_gu, :] = gu_part(0, half)

    def gu_finish():
        for half in (0, 1):
            rows = slice(half * half_gu, (half + 1) * half_gu)
            a, b = (2, 4) if half == 0 else (1, 5)
            gu_hop(a).wait_recv()
            gu_hop(b).wait_recv()
            gu_out[rows, :] = (gu_out[rows, :] + gu_come[a].astype(F32) + gu_come[b].astype(F32)) * scale

    gu_send(0)
    gu_send(3)

    later = (
        lax.broadcasted_iota(jnp.int32, (tok, tok), 1) < lax.broadcasted_iota(jnp.int32, (tok, tok), 0)
    ).astype(BF16)
    lane = lax.broadcasted_iota(jnp.int32, (tok, LANES), 1)
    expert_lane = jnp.where(lane < PEERS, (lane // NC) * (NZ * NC) + z * NC + lax.rem(lane, NC), -1).astype(F32)
    slot_lane = lax.broadcasted_iota(jnp.int32, (tok, pad), 1).astype(F32)

    def spread_one(s, _):
        side = side_ref[s].astype(F32)
        match = jnp.zeros((tok, LANES), F32)
        for k in range(TOP):
            match = match + (jnp.broadcast_to(side[:, k : k + 1], (tok, LANES)) == expert_lane).astype(F32)
        position = jnp.dot(later, match.astype(BF16), preferred_element_type=F32)
        slot = jnp.where(match > 0.0, position + (s * cap).astype(F32), -1.0)
        for peer in range(PEERS):
            hit = jnp.broadcast_to(slot[:, peer : peer + 1], (tok, pad)) == slot_lane
            spread[s, :, peer * pad : (peer + 1) * pad] = hit.astype(F32).astype(BF16)
        return 0

    lax.fori_loop(0, NZ, spread_one, 0)

    def x_arrived(ch):
        def one(step, _):
            peer = lax.rem(me + step, PEERS)
            for copy in x_copies(ch, peer, peer, peer, peer):
                copy.wait_recv()
            return 0

        lax.fori_loop(1, PEERS, one, 0)
        for copy in own_copies(ch):
            copy.wait()

    def combines(ch, lo, hi):
        def one(k, _):
            width = chunks[ch][1]
            s = lax.rem(z + NZ // 2 + k, NZ)
            rows = spread[s]
            for at in range(0, width, 256):
                w = min(256, width - at)
                cols = landed[ch][:, :, at : at + w].reshape(PEERS * pad, w)
                total[ch][s, :, at : at + w] = jnp.dot(rows, cols, preferred_element_type=F32)
            return 0

        lax.fori_loop(lo, hi, one, 0)

    def hop(ch, way, i):
        step = 1 + way * (NZ - 2)
        return pltpu.make_async_remote_copy(
            src_ref=leave[ch].at[way, i],
            dst_ref=come[ch].at[way, i],
            send_sem=z_send.at[ch, way, i],
            recv_sem=z_recv.at[ch, way, i],
            device_id=device(x, lax.rem(z + step, NZ), c),
            device_id_type=MESH,
        )

    def z_step(ch, i):
        dist = NZ // 2 - (i + 1) // 2

        def one(way, _):
            s = lax.rem(z + (1 + way * (NZ - 2)) * dist, NZ)
            half = lax.rem(i + way, 2)
            value = total[ch][s, aligned(half, half_rows), :]
            if i >= 2:
                hop(ch, way, i - 2).wait_recv()
                value = value + come[ch][way, i - 2].astype(F32)
            leave[ch][way, i] = value.astype(BF16)
            hop(ch, way, i).start()
            return 0

        lax.fori_loop(0, 2, one, 0)

    def finish(ch):
        for way in (0, 1):
            hop(ch, way, sends - 2).wait_recv()
            hop(ch, way, sends - 1).wait_recv()
        for half in (0, 1):
            rows = slice(half * half_rows, (half + 1) * half_rows)
            value = total[ch][z, rows, :]
            for way in (0, 1):
                i = sends - 1 if (sends - 1 + way) % 2 == half else sends - 2
                value = value + come[ch][way, i].astype(F32)
            for array, col, w, off in chunks[ch][0]:
                outs[array][rows, col : col + w] = value[:, off : off + w].astype(BF16)

    x_start(2)
    x_arrived(0)
    combines(0, 0, NZ)
    period = NZ // 2
    extra = {
        0: ((gu_send, 1), (gu_send, 4)),
        1: ((gu_send, 2), (gu_send, 5)),
        2: ((gu_own, 0), (gu_own, 1)),
    }
    for tick in range(period * (n - 1) + sends):
        ch, r = divmod(tick, period)
        for k, i in ((ch - 1, r + period), (ch, r)):
            if 0 <= k < n and i < sends:
                z_step(k, i)
        if ch < n:
            if r == 0 and ch + 1 < n:
                x_arrived(ch + 1)
                if ch + 3 < n:
                    x_start(ch + 3)
            if ch + 1 < n:
                combines(ch + 1, NZ * r // period, NZ * (r + 1) // period)
            if r == 1 and ch > 1:
                finish(ch - 2)
            if r in (1, 3) and ch in extra:
                work, arg = extra[ch][r // 2]
                work(arg)
    finish(n - 2)
    finish(n - 1)
    gu_finish()
    for ch in range(n):

        def drain(i, _, ch=ch):
            for way in (0, 1):
                hop(ch, way, i).wait_send()
            return 0

        lax.fori_loop(0, sends, drain, 0)

        def sent(step, _, ch=ch):
            peer = lax.rem(me + step, PEERS)
            for copy in x_copies(ch, peer, me, me, peer):
                copy.wait_send()
            return 0

        lax.fori_loop(1, PEERS, sent, 0)
    for k in range(6):
        gu_hop(k).wait_send()


def back(side, gate_rows, rows, x_rows, pre, cap, gu_rows, scale):
    width = rows.shape[2]
    tok = side.shape[1]
    pad = -(-NZ * cap // LANES) * LANES
    chunks, col = [], 0
    for w in BACK_CHUNKS:
        off = 0 if chunks else LANES
        chunks.append(([(0, 0, LANES, 0)] * (off > 0) + [(1, col, w, off)], off + w))
        col += w
    n = len(chunks)
    vmem = pl.BlockSpec(memory_space=pltpu.VMEM)
    shape = jax.ShapeDtypeStruct
    return pl.pallas_call(
        functools.partial(back_kernel, chunks, cap, scale),
        out_shape=(shape((tok, LANES), BF16), shape((tok, width), BF16), shape((gu_rows, pre.shape[1]), F32)),
        in_specs=[vmem] * 5,
        out_specs=(vmem,) * 3,
        scratch_shapes=[pltpu.VMEM((PEERS, pad, w), BF16) for _, w in chunks]
        + [pltpu.VMEM((NZ, tok, w), F32) for _, w in chunks]
        + [pltpu.VMEM((2, NZ - 1, tok // 2, w), BF16) for _, w in chunks] * 2
        + [
            pltpu.VMEM((NZ, tok, PEERS * pad), BF16),
            pltpu.VMEM((6, gu_rows // 2, pre.shape[1]), BF16),
            pltpu.VMEM((6, gu_rows // 2, pre.shape[1]), BF16),
            pltpu.SemaphoreType.DMA((n, 2, NZ - 1)),
            pltpu.SemaphoreType.DMA((n, 2, NZ - 1)),
            pltpu.SemaphoreType.DMA((n, 2, PEERS)),
            pltpu.SemaphoreType.DMA((n, 2, PEERS)),
            pltpu.SemaphoreType.DMA((n, 2)),
            pltpu.SemaphoreType.DMA((6,)),
            pltpu.SemaphoreType.DMA((6,)),
        ],
        compiler_params=pltpu.CompilerParams(collective_id=1, has_side_effects=True, vmem_limit_bytes=62 << 20),
        cost_estimate=pl.CostEstimate(flops=10_000_000_000, bytes_accessed=250_000_000, transcendentals=0),
        name="back",
    )(side, gate_rows, rows, x_rows, pre)


def on_device(tokens, out_grad, routes, gate_weights, saved_preacts, gate_up, down_proj):
    groups = lax.axis_size("dp")
    tok_rows, top = routes.shape
    cap = saved_preacts.shape[2] // lax.axis_size("expert")
    zeros = functools.partial(jnp.zeros, dtype=BF16)
    side = jnp.concatenate(
        [
            routes.T.astype(BF16),
            zeros((GATE_LANE - top, tok_rows)),
            gate_weights.T,
            zeros((LANES - GATE_LANE - top, tok_rows)),
        ]
    )
    grad_scale = float(1.0 / (groups * tok_rows * top) ** 0.5)
    sides, x_rows, pre, gate_rows, rows, grad_dn = front(
        side, out_grad, tokens, saved_preacts[0, 0], gate_up[0], down_proj[0], cap, grad_scale
    )
    gates, grad_tokens, grad_gu = back(sides, gate_rows, rows, x_rows, pre, cap, gate_up.shape[1], grad_scale)
    return (grad_tokens, gates[:, :top], grad_gu[None], grad_dn[None])


def solution(mesh):
    in_specs = (
        P(("dp", "expert"), None),
        P(("dp", "expert"), None),
        P(("dp", "expert"), None),
        P(("dp", "expert"), None),
        P("dp", "expert", None, None),
        P("expert", "dp", None),
        P("expert", "dp", None),
    )
    out_specs = (
        P(("dp", "expert"), None),
        P(("dp", "expert"), None),
        P("expert", "dp", None),
        P("expert", "dp", None),
    )
    return jax.shard_map(
        on_device, mesh=mesh, in_specs=in_specs, out_specs=out_specs, check_vma=False
    )
```

```python
import functools

import jax
import jax.numpy as jnp
from jax import lax
from jax.experimental import pallas as pl
from jax.experimental.pallas import tpu as pltpu
from jax.sharding import PartitionSpec as P

MESH = pl.DeviceIdType.MESH
BF16, F32 = jnp.bfloat16, jnp.float32
NX, NZ, NC = 4, 8, 2
NY = 4
PEERS = NX * NC
LANES = 128
TOP = 6
DY_CHUNKS, X_CHUNKS = (512, 768, 768), (768, 768, 512)
BACK_CHUNKS = (256, 384, 512, 512, 384)
GATE_LANE = 8
NT = (((1,), (1,)), ((), ()))
TN = (((0,), (0,)), ((), ()))


def place():
    e = lax.axis_index("expert")
    return e // (NZ * NC), lax.rem(e // NC, NZ), lax.rem(e, NC)


def device(x, z, c):
    return (lax.axis_index("dp"), (x * NZ + z) * NC + c)


def along_y(step):
    return (lax.rem(lax.axis_index("dp") + step, NY), lax.axis_index("expert"))


def enter(x, z, c):
    barrier = pltpu.get_barrier_semaphore()
    for step in (1, NZ - 1):
        pl.semaphore_signal(barrier, inc=1, device_id=device(x, lax.rem(z + step, NZ), c), device_id_type=MESH)
    for step in (1, NY - 1):
        pl.semaphore_signal(barrier, inc=1, device_id=along_y(step), device_id_type=MESH)
    me = x * NC + c
    for step in range(1, PEERS):
        peer = lax.rem(me + step, PEERS)
        pl.semaphore_signal(barrier, inc=1, device_id=device(peer // NC, z, lax.rem(peer, NC)), device_id_type=MESH)
    pl.semaphore_wait(barrier, 2 + 2 + PEERS - 1)


def aligned(index, size):
    return pl.ds(pl.multiple_of(index * size, size), size)


def front_kernel(
    chunks,
    cap,
    scale,
    side_in,
    dy_in,
    x_in,
    saved,
    up_in,
    down_in,
    side_out,
    x_out,
    pre_hbm,
    gate_out,
    row_hbm,
    dn_out,
    *scratch,
):
    n = len(chunks)
    ring, stage = scratch[:n], scratch[n : n + n // 2] * 2
    later = scratch[n + n // 2 :]
    side_own, side_rows, dy_rows, scaled_rows, pick, up, down, act, turned_act, coef_gate, coef_up, dn, dn_come, dn_sum, pre_out, row_out = later[:16]
    z_send, z_recv, x_send, x_recv, own_sem, y_send, y_recv, y_own, d_send, d_recv, w_sem = later[16:]
    ins, outs = (side_own, dy_in, x_in), (side_rows, dy_rows, x_out)
    x, z, c = place()
    y = lax.axis_index("dp")
    expert = lax.axis_index("expert")
    me = x * NC + c
    tok, width = dy_in.shape
    half_rows = tok // 2
    block = pick.shape[1]
    padded = dy_rows.shape[1]
    hidden = act.shape[1]
    sends = NZ - 1
    unit = NC * padded

    eye = (lax.broadcasted_iota(jnp.int32, (tok, tok), 0) == lax.broadcasted_iota(jnp.int32, (tok, tok), 1)).astype(BF16)
    side_own[...] = lax.dot_general(eye, side_in[...], NT, preferred_element_type=F32).astype(BF16)
    for segments, buf in ((s, b) for (s, _), b in zip(chunks, ring)):
        for array, col, w, off in segments:
            buf[z, :, off : off + w] = ins[array][:, col : col + w]
    for buf in outs[:2]:
        buf[:, block:, :] = jnp.zeros((PEERS, padded - block, buf.shape[2]), BF16)
    enter(x, z, c)

    weights = ((down_in, down), (up_in, up))

    def y_copy(k, hop):
        source, whole = weights[k]
        rows = whole.shape[1]
        cut = rows // 32 * 16
        first, second = (0, cut), (cut, rows - cut)
        lo, size = (first, second, second, first, first, second)[hop]
        step = 1 if hop in (0, 1, 4) else NY - 1
        back = NY - step
        slot = y if hop < 4 else lax.rem(y + back, NY)
        src = source.at[lo : lo + size, :] if hop < 4 else whole.at[slot, lo : lo + size, :]
        return pltpu.make_async_remote_copy(
            src_ref=src,
            dst_ref=whole.at[slot, lo : lo + size, :],
            send_sem=y_send.at[k, hop],
            recv_sem=y_recv.at[k, hop],
            device_id=along_y(step),
            device_id_type=MESH,
        )

    def y_own_copy(k):
        return pltpu.make_async_copy(weights[k][0], weights[k][1].at[y], y_own.at[k])

    def y_forward(k):
        y_copy(k, 0).wait_recv()
        y_copy(k, 4).start()
        y_copy(k, 2).wait_recv()
        y_copy(k, 5).start()

    def y_arrived(k):
        for hop in (1, 3, 4, 5):
            y_copy(k, hop).wait_recv()
        y_own_copy(k).wait()

    def hop(ch, way, i):
        step = 1 if way == 0 else NZ - 1
        dist = i // 2
        half = lax.rem(i + way, 2)
        blk = lax.rem(z + (NZ - step) * dist, NZ)
        view = ring[ch].at[blk, aligned(half, half_rows), :]
        return pltpu.make_async_remote_copy(
            src_ref=view,
            dst_ref=view,
            send_sem=z_send.at[ch, way, i],
            recv_sem=z_recv.at[ch, way, i],
            device_id=device(x, lax.rem(z + step, NZ), c),
            device_id_type=MESH,
        )

    def z_start(ch, i):
        for way in (0, 1):
            hop(ch, way, i).start()

    def z_arrived(ch, i):
        for way in (0, 1):
            hop(ch, way, i).wait_recv()

    def x_copies(ch, peer, slot, mark):
        made = []
        for array, col, w, off in chunks[ch][0]:
            kind = 0 if array == 0 else 1
            made.append(
                pltpu.make_async_remote_copy(
                    src_ref=stage[ch].at[peer, :, off : off + w],
                    dst_ref=outs[array].at[slot, 0:block, col : col + w],
                    send_sem=x_send.at[ch, kind, peer],
                    recv_sem=x_recv.at[ch, kind, mark],
                    device_id=device(peer // NC, z, lax.rem(peer, NC)),
                    device_id_type=MESH,
                )
            )
        return made

    def own_copies(ch):
        return [
            pltpu.make_async_copy(
                stage[ch].at[me, :, off : off + w],
                outs[array].at[me, 0:block, col : col + w],
                own_sem.at[ch, 0 if array == 0 else 1],
            )
            for array, col, w, off in chunks[ch][0]
        ]

    def make_pick():
        earlier = (
            lax.broadcasted_iota(jnp.int32, (tok, tok), 0) < lax.broadcasted_iota(jnp.int32, (tok, tok), 1)
        ).astype(BF16)
        slot_row = lax.broadcasted_iota(jnp.int32, (block, tok), 0).astype(F32)
        peer_row = lax.broadcasted_iota(jnp.int32, (PEERS, tok), 0)
        expert_row = ((peer_row // NC) * (NZ * NC) + z * NC + lax.rem(peer_row, NC)).astype(F32)
        turn = (
            lax.broadcasted_iota(jnp.int32, (LANES, LANES), 0) == lax.broadcasted_iota(jnp.int32, (LANES, LANES), 1)
        ).astype(BF16)

        def one(s, _):
            turned = lax.dot_general(turn, ring[0][s, :, 0:LANES], NT, preferred_element_type=F32)
            match = jnp.zeros((PEERS, tok), F32)
            for k in range(TOP):
                match = match + (jnp.broadcast_to(turned[k : k + 1, :], (PEERS, tok)) == expert_row).astype(F32)
            position = jnp.dot(match.astype(BF16), earlier, preferred_element_type=F32)
            slot = jnp.where(match > 0.0, position + (s * cap).astype(F32), -1.0)
            for peer in range(PEERS):
                hit = jnp.broadcast_to(slot[peer : peer + 1, :], (block, tok)) == slot_row
                pick[peer, :, aligned(s, tok)] = hit.astype(F32).astype(BF16)
            return 0

        lax.fori_loop(0, NZ, one, 0)
        side_out[...] = ring[0][:, :, 0:LANES]

    def pieces(ch, lo, hi):
        def one(peer, _):
            w_all = chunks[ch][1]
            rows = pick[peer]
            for at in range(0, w_all, 256):
                w = min(256, w_all - at)
                cols = ring[ch][:, :, at : at + w].reshape(NZ * tok, w)
                stage[ch][peer, :, at : at + w] = jnp.dot(rows, cols, preferred_element_type=F32).astype(BF16)

            @pl.when(peer != me)
            def _():
                for copy in x_copies(ch, peer, me, me):
                    copy.start()

            @pl.when(peer == me)
            def _():
                for copy in own_copies(ch):
                    copy.start()

            return 0

        lax.fori_loop(lo, hi, one, 0)

    per_x = NZ * NC * cap
    new = lax.broadcasted_iota(jnp.int32, (unit, per_x), 0)
    old = lax.broadcasted_iota(jnp.int32, (unit, per_x), 1)
    core = (new >= padded).astype(jnp.int32)
    inner = new - core * padded

    def prepare(b):
        order = jnp.zeros((unit, per_x), jnp.bool_)
        for zed in range(NZ):
            order = order | (
                (inner >= zed * cap) & (inner < (zed + 1) * cap) & (old == inner + zed * (NC - 1) * cap + core * cap)
            )
        moved = jnp.dot(order.astype(F32).astype(BF16), saved[aligned(b, per_x), :], preferred_element_type=F32)
        gate, lift = moved[:, :hidden], moved[:, hidden:]
        sig = jax.nn.sigmoid(gate)
        rows = aligned(b, unit)
        swish = gate * sig
        act[rows, :] = (swish * lift).astype(BF16)
        coef_gate[rows, :] = lift * sig * (1.0 + gate * (1.0 - sig))
        coef_up[rows, :] = swish

    def gain_of(b):
        side = side_rows[pl.ds(b * NC, NC), :, :].reshape(unit, LANES).astype(F32)
        mine = expert.astype(F32)
        gain = jnp.zeros((unit, 1), F32)
        for k in range(TOP):
            gain = gain + jnp.where(side[:, k : k + 1] == mine, side[:, GATE_LANE + k : GATE_LANE + k + 1], 0.0)
        return side, mine, gain

    def scale_rows(b):
        two = pl.ds(b * NC, NC)
        gain = gain_of(b)[2]
        for at in range(0, width, 512):
            part = dy_rows[two, :, at : at + 512].reshape(unit, 512).astype(F32)
            scaled_rows[two, :, at : at + 512] = (gain * part).astype(BF16).reshape(NC, padded, 512)

    def pre_copy(b):
        rows = aligned(b, unit)
        return pltpu.make_async_copy(pre_out.at[rows, :], pre_hbm.at[rows, :], w_sem.at[0, b])

    def row_copy(b):
        two = pl.ds(b * NC, NC)
        return pltpu.make_async_copy(row_out.at[two], row_hbm.at[two], w_sem.at[1, b])

    def through_down(b):
        rows = aligned(b, unit)
        two = pl.ds(b * NC, NC)
        dy = dy_rows[two, :, :].reshape(unit, width)
        act_grad = lax.dot_general(dy, down[...].reshape(hidden, width), NT, preferred_element_type=F32)
        gate_grad = jnp.sum(act[rows, :].astype(F32) * act_grad, axis=1, keepdims=True) / jnp.sqrt(F32(width))
        side, mine, gain = gain_of(b)
        lane = lax.broadcasted_iota(jnp.int32, (unit, LANES), 1)
        gate_out[two, :, :] = (
            jnp.where((lane < TOP) & (side == mine), jnp.broadcast_to(gate_grad, (unit, LANES)), 0.0)
            .astype(BF16)
            .reshape(NC, padded, LANES)
        )
        scaled = gain * act_grad
        pre_out[rows, 0:hidden] = (scaled * coef_gate[rows, :]).astype(BF16)
        pre_out[rows, hidden : 2 * hidden] = (scaled * coef_up[rows, :]).astype(BF16)
        pre_copy(b).start()

    def through_up(b):
        rows = aligned(b, unit)
        two = pl.ds(b * NC, NC)

        def one(q, _):
            grad = lax.dot_general(pre_out[rows, :], up[q], NT, preferred_element_type=F32)
            row_out[two, :, aligned(q, up.shape[1])] = grad.astype(BF16).reshape(NC, padded, up.shape[1])
            return 0

        lax.fori_loop(0, NY, one, 0)
        row_copy(b).start()

    def down_grad(k):
        cols = aligned(k, 512)
        scaled_dy = scaled_rows[:, :, cols].reshape(PEERS * padded, 512)
        dn[:, :, cols] = (
            jnp.dot(turned_act[...], scaled_dy, preferred_element_type=F32).astype(BF16).reshape(NY, hidden // NY, 512)
        )

    dn_rows = hidden // NY
    dn_cut = dn_rows // 32 * 16
    spans = ((0, dn_cut), (dn_cut, dn_rows - dn_cut))

    def dn_hop(k):
        lo, size = spans[(0, 1, 0, 1, 0, 1)[k]]
        src = dn_sum.at[k // 3, 0:size, :]
        if k in (0, 1, 3, 4):
            ahead = (2, 1, 0, 2, NY - 1)[k]
            src = dn.at[lax.rem(y + ahead, NY), lo : lo + size, :]
        return pltpu.make_async_remote_copy(
            src_ref=src,
            dst_ref=dn_come.at[k, 0:size, :],
            send_sem=d_send.at[k],
            recv_sem=d_recv.at[k],
            device_id=along_y(1 if k < 3 else NY - 1),
            device_id_type=MESH,
        )

    def dn_pass_on():
        for k in (2, 5):
            lo, size = spans[0 if k == 2 else 1]
            dn_hop(k - 2).wait_recv()
            own = dn[lax.rem(y + (1 if k == 2 else NY - 1), NY), lo : lo + size, :].astype(F32)
            dn_sum[k // 3, 0:size, :] = (own + dn_come[k - 2, 0:size, :].astype(F32)).astype(BF16)
            dn_hop(k).start()

    def dn_finish():
        for (lo, size), (a, b) in zip(spans, ((2, 4), (1, 5))):
            dn_hop(a).wait_recv()
            dn_hop(b).wait_recv()
            value = dn[y, lo : lo + size, :].astype(F32)
            value = value + dn_come[a, 0:size, :].astype(F32) + dn_come[b, 0:size, :].astype(F32)
            dn_out[lo : lo + size, :] = value * scale

    def run(work, lo, hi):
        def one(b, _):
            work(b)
            return 0

        lax.fori_loop(lo, hi, one, 0)

    for k in (0, 1):
        y_own_copy(k).start()
        for h in (0, 2, 1, 3):
            y_copy(k, h).start()
    ticks = sends - 2
    half_n = n // 2

    def drained(ch):
        def sent(step, _):
            peer = lax.rem(me + step, PEERS)
            for copy in x_copies(ch, peer, me, me):
                copy.wait_send()
            return 0

        lax.fori_loop(1, PEERS, sent, 0)

    def own_landed(ch):
        for copy in own_copies(ch):
            copy.wait()

    def free_stage(ch):
        if ch >= half_n:
            drained(ch - half_n)

    def x_landed(ch):
        def one(step, _):
            peer = lax.rem(me + step, PEERS)
            for copy in x_copies(ch, peer, peer, peer):
                copy.wait_recv()
            return 0

        lax.fori_loop(1, PEERS, one, 0)

    z_start(0, 0)
    z_start(0, 1)
    for ch in range(n):
        if ch > 0:
            z_arrived(ch - 1, sends - 2)
            z_arrived(ch - 1, sends - 1)
            free_stage(ch - 1)
        if ch > 1:
            own_landed(ch - 2)
        if ch == 1:
            make_pick()
        if ch in (2, 3):
            y_forward(ch - 2)

        def tick(i, _, ch=ch):
            z_arrived(ch, i)
            z_start(ch, i + 2)
            if ch + 1 < n:

                @pl.when(i >= ticks - 2)
                def _():
                    z_start(ch + 1, i - (ticks - 2))

            if ch == 0:
                run(prepare, (NX * i) // ticks, (NX * (i + 1)) // ticks)
            else:
                pieces(ch - 1, jnp.minimum(4 * i, PEERS), jnp.minimum(4 * i + 4, PEERS))
            if ch == half_n + 1:

                @pl.when(i == 2)
                def _():
                    for k in range(half_n):
                        x_landed(k)
                    run(scale_rows, 0, NX)

                tiles = width // 512
                run(down_grad, jnp.clip(2 * (i - 3), 0, tiles), jnp.clip(2 * (i - 2), 0, tiles))
            if ch == n - 1:

                @pl.when(i == 0)
                def _():
                    y_arrived(0)

                run(through_down, jnp.maximum(i - 1, 0), i)
            return 0

        lax.fori_loop(0, ticks, tick, 0)
        if ch == 0:
            turned_act[...] = act[...].astype(F32).T.astype(BF16)
        if ch == half_n + 1:
            for k in (0, 3, 1, 4):
                dn_hop(k).start()
    z_arrived(n - 1, sends - 2)
    z_arrived(n - 1, sends - 1)
    free_stage(n - 1)
    pieces(n - 1, 0, PEERS)
    dn_pass_on()
    y_arrived(1)
    run(through_up, 0, NX)
    dn_finish()
    for ch in range(n):
        if ch >= half_n:
            x_landed(ch)
            drained(ch)
        if ch >= n - 2:
            own_landed(ch)

        def drain(i, _, ch=ch):
            for way in (0, 1):
                hop(ch, way, i).wait_send()
            return 0

        lax.fori_loop(0, sends, drain, 0)
    for b in range(NX):
        pre_copy(b).wait()
        row_copy(b).wait()
    for k in (0, 1):
        for h in range(6):
            y_copy(k, h).wait_send()
    for k in range(6):
        dn_hop(k).wait_send()


def front(side, dy, x, saved, up, down, cap, scale):
    tok, width = dy.shape
    hidden = up.shape[1] // 2
    block = NZ * cap
    padded = -(-block // 16) * 16
    chunks = []
    for array, widths in ((1, DY_CHUNKS), (2, X_CHUNKS)):
        col = 0
        for w in widths:
            off = 0 if chunks else LANES
            chunks.append(([(0, 0, LANES, 0)] * (off > 0) + [(array, col, w, off)], off + w))
            col += w
    n = len(chunks)
    rows = PEERS * padded
    dn_part = hidden // NY - hidden // NY // 32 * 16
    vmem = pl.BlockSpec(memory_space=pltpu.VMEM)
    anywhere = pl.BlockSpec(memory_space=pl.ANY)
    shape = jax.ShapeDtypeStruct
    return pl.pallas_call(
        functools.partial(front_kernel, chunks, cap, scale),
        out_shape=(
            shape((NZ, tok, LANES), BF16),
            shape((PEERS, padded, width), BF16),
            shape((rows, 2 * hidden), BF16),
            shape((PEERS, padded, LANES), BF16),
            shape((PEERS, padded, width), BF16),
            shape((hidden // NY, width), F32),
        ),
        in_specs=[vmem] * 4 + [anywhere] * 2,
        out_specs=(vmem, anywhere, anywhere, vmem, anywhere, vmem),
        scratch_shapes=[pltpu.VMEM((NZ, tok, w), BF16) for _, w in chunks]
        + [pltpu.VMEM((PEERS, block, max(a[1], b[1])), BF16) for a, b in zip(chunks[: n // 2], chunks[n // 2 :])]
        + [
            pltpu.VMEM((tok, LANES), BF16),
            pltpu.VMEM((PEERS, padded, LANES), BF16),
            pltpu.VMEM((PEERS, padded, width), BF16),
            pltpu.VMEM((PEERS, padded, width), BF16),
            pltpu.VMEM((PEERS, block, NZ * tok), BF16),
            pltpu.VMEM((NY,) + up.shape, BF16),
            pltpu.VMEM((NY,) + down.shape, BF16),
            pltpu.VMEM((rows, hidden), BF16),
            pltpu.VMEM((hidden, rows), BF16),
            pltpu.VMEM((rows, hidden), F32),
            pltpu.VMEM((rows, hidden), F32),
            pltpu.VMEM((NY, hidden // NY, width), BF16),
            pltpu.VMEM((6, dn_part, width), BF16),
            pltpu.VMEM((2, dn_part, width), BF16),
            pltpu.VMEM((rows, 2 * hidden), BF16),
            pltpu.VMEM((PEERS, padded, width), BF16),
            pltpu.SemaphoreType.DMA((n, 2, NZ - 1)),
            pltpu.SemaphoreType.DMA((n, 2, NZ - 1)),
            pltpu.SemaphoreType.DMA((n, 2, PEERS)),
            pltpu.SemaphoreType.DMA((n, 2, PEERS)),
            pltpu.SemaphoreType.DMA((n, 2)),
            pltpu.SemaphoreType.DMA((2, 6)),
            pltpu.SemaphoreType.DMA((2, 6)),
            pltpu.SemaphoreType.DMA((2,)),
            pltpu.SemaphoreType.DMA((6,)),
            pltpu.SemaphoreType.DMA((6,)),
            pltpu.SemaphoreType.DMA((2, NX)),
        ],
        compiler_params=pltpu.CompilerParams(collective_id=0, has_side_effects=True, vmem_limit_bytes=62 << 20),
        cost_estimate=pl.CostEstimate(flops=20_000_000_000, bytes_accessed=350_000_000, transcendentals=0),
        name="front",
    )(side, dy, x, saved, up, down)


def back_kernel(
    chunks, cap, scale, side_ref, gate_ref, row_ref, x_hbm, pre_hbm, gate_out, tok_out, gu_out, *scratch
):
    n = len(chunks)
    landed, total, leave, come = (scratch[k * n : (k + 1) * n] for k in range(4))
    spread, gu_leave, gu_come, x_ref, pre_ref, z_send, z_recv, x_send, x_recv, own_sem, y_send, y_recv, in_sem = scratch[4 * n :]
    ins, outs = (gate_ref, row_ref), (gate_out, tok_out)
    x, z, c = place()
    y = lax.axis_index("dp")
    me = x * NC + c
    tok = tok_out.shape[0]
    half_rows = tok // 2
    block = NZ * cap
    padded = row_ref.shape[1]
    pad = landed[0].shape[1]
    sends = NZ - 1

    x_ref[:, block:, :] = jnp.zeros((PEERS, padded - block, x_ref.shape[2]), BF16)
    fetches = (
        pltpu.make_async_copy(x_hbm.at[:, 0:block, :], x_ref.at[:, 0:block, :], in_sem.at[0]),
        pltpu.make_async_copy(pre_hbm, pre_ref, in_sem.at[1]),
    )
    for copy in fetches:
        copy.start()
    for buf, (_, w) in zip(landed, chunks):
        buf[:, block:, :] = jnp.zeros((PEERS, pad - block, w), BF16)
    enter(x, z, c)

    def x_copies(ch, src_slot, dst_slot, mark, peer):
        made = []
        for array, col, w, off in chunks[ch][0]:
            made.append(
                pltpu.make_async_remote_copy(
                    src_ref=ins[array].at[src_slot, 0:block, col : col + w],
                    dst_ref=landed[ch].at[dst_slot, 0:block, off : off + w],
                    send_sem=x_send.at[ch, array, peer],
                    recv_sem=x_recv.at[ch, array, mark],
                    device_id=device(peer // NC, z, lax.rem(peer, NC)),
                    device_id_type=MESH,
                )
            )
        return made

    def own_copies(ch):
        return [
            pltpu.make_async_copy(
                ins[array].at[me, 0:block, col : col + w], landed[ch].at[me, 0:block, off : off + w], own_sem.at[ch, array]
            )
            for array, col, w, off in chunks[ch][0]
        ]

    def x_start(ch):
        def send(step, _):
            peer = lax.rem(me + step, PEERS)
            for copy in x_copies(ch, peer, me, me, peer):
                copy.start()
            return 0

        lax.fori_loop(1, PEERS, send, 0)
        for copy in own_copies(ch):
            copy.start()

    x_start(0)
    x_start(1)

    gu_rows = gu_out.shape[0]
    half_gu = gu_rows // 2

    def gu_part(ahead, half):
        first = lax.rem(y + ahead, NY) * gu_rows + half * half_gu
        cols = x_ref[:, :, pl.ds(pl.multiple_of(first, half_gu), half_gu)].reshape(PEERS * padded, half_gu)
        return lax.dot_general(cols, pre_ref[...], TN, preferred_element_type=F32)

    def gu_hop(k):
        return pltpu.make_async_remote_copy(
            src_ref=gu_leave.at[k],
            dst_ref=gu_come.at[k],
            send_sem=y_send.at[k],
            recv_sem=y_recv.at[k],
            device_id=along_y(1 if k < 3 else NY - 1),
            device_id_type=MESH,
        )

    def gu_send(k):
        up = k < 3
        ahead = 2 if k in (0, 3) else (1 if up else NY - 1)
        half = (0 if up else 1) if k in (0, 2, 3, 5) else (1 if up else 0)
        value = gu_part(ahead, half)
        if k in (2, 5):
            gu_hop(k - 2).wait_recv()
            value = value + gu_come[k - 2].astype(F32)
        gu_leave[k] = value.astype(BF16)
        gu_hop(k).start()

    def gu_own(half):
        gu_out[half * half_gu : (half + 1) * half_gu, :] = gu_part(0, half)

    def gu_finish():
        for half in (0, 1):
            rows = slice(half * half_gu, (half + 1) * half_gu)
            a, b = (2, 4) if half == 0 else (1, 5)
            gu_hop(a).wait_recv()
            gu_hop(b).wait_recv()
            gu_out[rows, :] = (gu_out[rows, :] + gu_come[a].astype(F32) + gu_come[b].astype(F32)) * scale

    for copy in fetches:
        copy.wait()
    gu_send(0)
    gu_send(3)

    later = (
        lax.broadcasted_iota(jnp.int32, (tok, tok), 1) < lax.broadcasted_iota(jnp.int32, (tok, tok), 0)
    ).astype(BF16)
    lane = lax.broadcasted_iota(jnp.int32, (tok, LANES), 1)
    expert_lane = jnp.where(lane < PEERS, (lane // NC) * (NZ * NC) + z * NC + lax.rem(lane, NC), -1).astype(F32)
    slot_lane = lax.broadcasted_iota(jnp.int32, (tok, pad), 1).astype(F32)

    def spread_one(s, _):
        side = side_ref[s].astype(F32)
        match = jnp.zeros((tok, LANES), F32)
        for k in range(TOP):
            match = match + (jnp.broadcast_to(side[:, k : k + 1], (tok, LANES)) == expert_lane).astype(F32)
        position = jnp.dot(later, match.astype(BF16), preferred_element_type=F32)
        slot = jnp.where(match > 0.0, position + (s * cap).astype(F32), -1.0)
        for peer in range(PEERS):
            hit = jnp.broadcast_to(slot[:, peer : peer + 1], (tok, pad)) == slot_lane
            spread[s, :, peer * pad : (peer + 1) * pad] = hit.astype(F32).astype(BF16)
        return 0

    lax.fori_loop(0, NZ, spread_one, 0)

    def x_arrived(ch):
        def one(step, _):
            peer = lax.rem(me + step, PEERS)
            for copy in x_copies(ch, peer, peer, peer, peer):
                copy.wait_recv()
            return 0

        lax.fori_loop(1, PEERS, one, 0)
        for copy in own_copies(ch):
            copy.wait()

    def combines(ch, lo, hi):
        def one(k, _):
            width = chunks[ch][1]
            s = lax.rem(z + NZ // 2 + k, NZ)
            rows = spread[s]
            for at in range(0, width, 256):
                w = min(256, width - at)
                cols = landed[ch][:, :, at : at + w].reshape(PEERS * pad, w)
                total[ch][s, :, at : at + w] = jnp.dot(rows, cols, preferred_element_type=F32)
            return 0

        lax.fori_loop(lo, hi, one, 0)

    def hop(ch, way, i):
        step = 1 + way * (NZ - 2)
        return pltpu.make_async_remote_copy(
            src_ref=leave[ch].at[way, i],
            dst_ref=come[ch].at[way, i],
            send_sem=z_send.at[ch, way, i],
            recv_sem=z_recv.at[ch, way, i],
            device_id=device(x, lax.rem(z + step, NZ), c),
            device_id_type=MESH,
        )

    def z_step(ch, i):
        dist = NZ // 2 - (i + 1) // 2

        def one(way, _):
            s = lax.rem(z + (1 + way * (NZ - 2)) * dist, NZ)
            half = lax.rem(i + way, 2)
            value = total[ch][s, aligned(half, half_rows), :]
            if i >= 2:
                hop(ch, way, i - 2).wait_recv()
                value = value + come[ch][way, i - 2].astype(F32)
            leave[ch][way, i] = value.astype(BF16)
            hop(ch, way, i).start()
            return 0

        lax.fori_loop(0, 2, one, 0)

    def finish(ch):
        for way in (0, 1):
            hop(ch, way, sends - 2).wait_recv()
            hop(ch, way, sends - 1).wait_recv()
        for half in (0, 1):
            rows = slice(half * half_rows, (half + 1) * half_rows)
            value = total[ch][z, rows, :]
            for way in (0, 1):
                i = sends - 1 if (sends - 1 + way) % 2 == half else sends - 2
                value = value + come[ch][way, i].astype(F32)
            for array, col, w, off in chunks[ch][0]:
                outs[array][rows, col : col + w] = value[:, off : off + w].astype(BF16)

    x_start(2)
    x_arrived(0)
    combines(0, 0, NZ)
    period = NZ // 2
    extra = {
        0: ((gu_send, 1), (gu_send, 4)),
        1: ((gu_send, 2), (gu_send, 5)),
        2: ((gu_own, 0), (gu_own, 1)),
    }
    for tick in range(period * (n - 1) + sends):
        ch, r = divmod(tick, period)
        for k, i in ((ch - 1, r + period), (ch, r)):
            if 0 <= k < n and i < sends:
                z_step(k, i)
        if ch < n:
            if r == 0 and ch + 1 < n:
                x_arrived(ch + 1)
                if ch + 3 < n:
                    x_start(ch + 3)
            if ch + 1 < n:
                combines(ch + 1, NZ * r // period, NZ * (r + 1) // period)
            if r == 1 and ch > 1:
                finish(ch - 2)
            if r in (1, 3) and ch in extra:
                work, arg = extra[ch][r // 2]
                work(arg)
    finish(n - 2)
    finish(n - 1)
    gu_finish()
    for ch in range(n):

        def drain(i, _, ch=ch):
            for way in (0, 1):
                hop(ch, way, i).wait_send()
            return 0

        lax.fori_loop(0, sends, drain, 0)

        def sent(step, _, ch=ch):
            peer = lax.rem(me + step, PEERS)
            for copy in x_copies(ch, peer, me, me, peer):
                copy.wait_send()
            return 0

        lax.fori_loop(1, PEERS, sent, 0)
    for k in range(6):
        gu_hop(k).wait_send()


def back(side, gate_rows, rows, x_rows, pre, cap, gu_rows, scale):
    width = rows.shape[2]
    tok = side.shape[1]
    pad = -(-NZ * cap // LANES) * LANES
    chunks, col = [], 0
    for w in BACK_CHUNKS:
        off = 0 if chunks else LANES
        chunks.append(([(0, 0, LANES, 0)] * (off > 0) + [(1, col, w, off)], off + w))
        col += w
    n = len(chunks)
    vmem = pl.BlockSpec(memory_space=pltpu.VMEM)
    shape = jax.ShapeDtypeStruct
    return pl.pallas_call(
        functools.partial(back_kernel, chunks, cap, scale),
        out_shape=(shape((tok, LANES), BF16), shape((tok, width), BF16), shape((gu_rows, pre.shape[1]), F32)),
        in_specs=[vmem, vmem] + [pl.BlockSpec(memory_space=pl.ANY)] * 3,
        out_specs=(vmem,) * 3,
        scratch_shapes=[pltpu.VMEM((PEERS, pad, w), BF16) for _, w in chunks]
        + [pltpu.VMEM((NZ, tok, w), F32) for _, w in chunks]
        + [pltpu.VMEM((2, NZ - 1, tok // 2, w), BF16) for _, w in chunks] * 2
        + [
            pltpu.VMEM((NZ, tok, PEERS * pad), BF16),
            pltpu.VMEM((6, gu_rows // 2, pre.shape[1]), BF16),
            pltpu.VMEM((6, gu_rows // 2, pre.shape[1]), BF16),
            pltpu.VMEM(x_rows.shape, BF16),
            pltpu.VMEM(pre.shape, BF16),
            pltpu.SemaphoreType.DMA((n, 2, NZ - 1)),
            pltpu.SemaphoreType.DMA((n, 2, NZ - 1)),
            pltpu.SemaphoreType.DMA((n, 2, PEERS)),
            pltpu.SemaphoreType.DMA((n, 2, PEERS)),
            pltpu.SemaphoreType.DMA((n, 2)),
            pltpu.SemaphoreType.DMA((6,)),
            pltpu.SemaphoreType.DMA((6,)),
            pltpu.SemaphoreType.DMA((2,)),
        ],
        compiler_params=pltpu.CompilerParams(collective_id=1, has_side_effects=True, vmem_limit_bytes=62 << 20),
        cost_estimate=pl.CostEstimate(flops=10_000_000_000, bytes_accessed=250_000_000, transcendentals=0),
        name="back",
    )(side, gate_rows, rows, x_rows, pre)


def on_device(tokens, out_grad, routes, gate_weights, saved_preacts, gate_up, down_proj):
    groups = lax.axis_size("dp")
    tok_rows, top = routes.shape
    cap = saved_preacts.shape[2] // lax.axis_size("expert")
    zeros = functools.partial(jnp.zeros, dtype=BF16)
    side = jnp.concatenate(
        [
            routes.T.astype(BF16),
            zeros((GATE_LANE - top, tok_rows)),
            gate_weights.T,
            zeros((LANES - GATE_LANE - top, tok_rows)),
        ]
    )
    grad_scale = float(1.0 / (groups * tok_rows * top) ** 0.5)
    sides, x_rows, pre, gate_rows, rows, grad_dn = front(
        side, out_grad, tokens, saved_preacts[0, 0], gate_up[0], down_proj[0], cap, grad_scale
    )
    gates, grad_tokens, grad_gu = back(sides, gate_rows, rows, x_rows, pre, cap, gate_up.shape[1], grad_scale)
    return (grad_tokens, gates[:, :top], grad_gu[None], grad_dn[None])


def solution(mesh):
    in_specs = (
        P(("dp", "expert"), None),
        P(("dp", "expert"), None),
        P(("dp", "expert"), None),
        P(("dp", "expert"), None),
        P("dp", "expert", None, None),
        P("expert", "dp", None),
        P("expert", "dp", None),
    )
    out_specs = (
        P(("dp", "expert"), None),
        P(("dp", "expert"), None),
        P("expert", "dp", None),
        P("expert", "dp", None),
    )
    return jax.shard_map(
        on_device, mesh=mesh, in_specs=in_specs, out_specs=out_specs, check_vma=False
    )
```

```python
import functools

import jax
import jax.numpy as jnp
from jax import lax
from jax.experimental import pallas as pl
from jax.experimental.pallas import tpu as pltpu
from jax.sharding import PartitionSpec as P

MESH = pl.DeviceIdType.MESH
BF16, F32 = jnp.bfloat16, jnp.float32
NX, NZ, NC = 4, 8, 2
NY = 4
PEERS = NX * NC
LANES = 128
TOP = 6
DY_CHUNKS, X_CHUNKS = (512, 768, 768), (768, 768, 512)
BACK_CHUNKS = (256, 384, 512, 512, 384)
GATE_LANE = 8
NT = (((1,), (1,)), ((), ()))
TN = (((0,), (0,)), ((), ()))


def place():
    e = lax.axis_index("expert")
    return e // (NZ * NC), lax.rem(e // NC, NZ), lax.rem(e, NC)


def device(x, z, c):
    return (lax.axis_index("dp"), (x * NZ + z) * NC + c)


def along_y(step):
    return (lax.rem(lax.axis_index("dp") + step, NY), lax.axis_index("expert"))


def enter(x, z, c):
    barrier = pltpu.get_barrier_semaphore()
    for step in (1, NZ - 1):
        pl.semaphore_signal(barrier, inc=1, device_id=device(x, lax.rem(z + step, NZ), c), device_id_type=MESH)
    for step in (1, NY - 1):
        pl.semaphore_signal(barrier, inc=1, device_id=along_y(step), device_id_type=MESH)
    me = x * NC + c
    for step in range(1, PEERS):
        peer = lax.rem(me + step, PEERS)
        pl.semaphore_signal(barrier, inc=1, device_id=device(peer // NC, z, lax.rem(peer, NC)), device_id_type=MESH)
    pl.semaphore_wait(barrier, 2 + 2 + PEERS - 1)


def aligned(index, size):
    return pl.ds(pl.multiple_of(index * size, size), size)


def front_kernel(
    chunks,
    cap,
    scale,
    side_in,
    dy_in,
    x_in,
    saved,
    up_in,
    down_in,
    side_out,
    x_out,
    pre_hbm,
    gate_out,
    row_hbm,
    dn_out,
    *scratch,
):
    n = len(chunks)
    ring, stage = scratch[:n], scratch[n : n + n // 2] * 2
    later = scratch[n + n // 2 :]
    side_own, side_rows, dy_rows, scaled_rows, pick, up, down, act, turned_act, coef_gate, coef_up, dn, dn_come, dn_sum, pre_out, row_out = later[:16]
    z_send, z_recv, x_send, x_recv, own_sem, y_send, y_recv, y_own, d_send, d_recv, w_sem = later[16:]
    ins, outs = (side_own, dy_in, x_in), (side_rows, dy_rows, x_out)
    x, z, c = place()
    y = lax.axis_index("dp")
    expert = lax.axis_index("expert")
    me = x * NC + c
    tok, width = dy_in.shape
    half_rows = tok // 2
    block = pick.shape[1]
    padded = dy_rows.shape[1]
    hidden = act.shape[1]
    sends = NZ - 1
    unit = NC * padded

    eye = (lax.broadcasted_iota(jnp.int32, (tok, tok), 0) == lax.broadcasted_iota(jnp.int32, (tok, tok), 1)).astype(BF16)
    side_own[...] = lax.dot_general(eye, side_in[...], NT, preferred_element_type=F32).astype(BF16)
    for segments, buf in ((s, b) for (s, _), b in zip(chunks, ring)):
        for array, col, w, off in segments:
            buf[z, :, off : off + w] = ins[array][:, col : col + w]
    for buf in outs[:2]:
        buf[:, block:, :] = jnp.zeros((PEERS, padded - block, buf.shape[2]), BF16)
    enter(x, z, c)

    weights = ((down_in, down), (up_in, up))

    def y_copy(k, hop):
        source, whole = weights[k]
        rows = whole.shape[1]
        cut = rows // 32 * 16
        first, second = (0, cut), (cut, rows - cut)
        lo, size = (first, second, second, first, first, second)[hop]
        step = 1 if hop in (0, 1, 4) else NY - 1
        back = NY - step
        slot = y if hop < 4 else lax.rem(y + back, NY)
        src = source.at[lo : lo + size, :] if hop < 4 else whole.at[slot, lo : lo + size, :]
        return pltpu.make_async_remote_copy(
            src_ref=src,
            dst_ref=whole.at[slot, lo : lo + size, :],
            send_sem=y_send.at[k, hop],
            recv_sem=y_recv.at[k, hop],
            device_id=along_y(step),
            device_id_type=MESH,
        )

    def y_own_copy(k):
        return pltpu.make_async_copy(weights[k][0], weights[k][1].at[y], y_own.at[k])

    def y_forward(k):
        y_copy(k, 0).wait_recv()
        y_copy(k, 4).start()
        y_copy(k, 2).wait_recv()
        y_copy(k, 5).start()

    def y_arrived(k):
        for hop in (1, 3, 4, 5):
            y_copy(k, hop).wait_recv()
        y_own_copy(k).wait()

    def hop(ch, way, i):
        step = 1 if way == 0 else NZ - 1
        dist = i // 2
        half = lax.rem(i + way, 2)
        blk = lax.rem(z + (NZ - step) * dist, NZ)
        view = ring[ch].at[blk, aligned(half, half_rows), :]
        return pltpu.make_async_remote_copy(
            src_ref=view,
            dst_ref=view,
            send_sem=z_send.at[ch, way, i],
            recv_sem=z_recv.at[ch, way, i],
            device_id=device(x, lax.rem(z + step, NZ), c),
            device_id_type=MESH,
        )

    def z_start(ch, i):
        for way in (0, 1):
            hop(ch, way, i).start()

    def z_arrived(ch, i):
        for way in (0, 1):
            hop(ch, way, i).wait_recv()

    def x_copies(ch, peer, slot, mark):
        made = []
        for array, col, w, off in chunks[ch][0]:
            kind = 0 if array == 0 else 1
            made.append(
                pltpu.make_async_remote_copy(
                    src_ref=stage[ch].at[peer, :, off : off + w],
                    dst_ref=outs[array].at[slot, 0:block, col : col + w],
                    send_sem=x_send.at[ch, kind, peer],
                    recv_sem=x_recv.at[ch, kind, mark],
                    device_id=device(peer // NC, z, lax.rem(peer, NC)),
                    device_id_type=MESH,
                )
            )
        return made

    def own_copies(ch):
        return [
            pltpu.make_async_copy(
                stage[ch].at[me, :, off : off + w],
                outs[array].at[me, 0:block, col : col + w],
                own_sem.at[ch, 0 if array == 0 else 1],
            )
            for array, col, w, off in chunks[ch][0]
        ]

    def make_pick():
        earlier = (
            lax.broadcasted_iota(jnp.int32, (tok, tok), 0) < lax.broadcasted_iota(jnp.int32, (tok, tok), 1)
        ).astype(BF16)
        slot_row = lax.broadcasted_iota(jnp.int32, (block, tok), 0).astype(F32)
        peer_row = lax.broadcasted_iota(jnp.int32, (PEERS, tok), 0)
        expert_row = ((peer_row // NC) * (NZ * NC) + z * NC + lax.rem(peer_row, NC)).astype(F32)
        turn = (
            lax.broadcasted_iota(jnp.int32, (LANES, LANES), 0) == lax.broadcasted_iota(jnp.int32, (LANES, LANES), 1)
        ).astype(BF16)

        def one(s, _):
            turned = lax.dot_general(turn, ring[0][s, :, 0:LANES], NT, preferred_element_type=F32)
            match = jnp.zeros((PEERS, tok), F32)
            for k in range(TOP):
                match = match + (jnp.broadcast_to(turned[k : k + 1, :], (PEERS, tok)) == expert_row).astype(F32)
            position = jnp.dot(match.astype(BF16), earlier, preferred_element_type=F32)
            slot = jnp.where(match > 0.0, position + (s * cap).astype(F32), -1.0)
            for peer in range(PEERS):
                hit = jnp.broadcast_to(slot[peer : peer + 1, :], (block, tok)) == slot_row
                pick[peer, :, aligned(s, tok)] = hit.astype(F32).astype(BF16)
            return 0

        lax.fori_loop(0, NZ, one, 0)
        side_out[...] = ring[0][:, :, 0:LANES]

    def pieces(ch, lo, hi):
        def one(peer, _):
            w_all = chunks[ch][1]
            rows = pick[peer]
            for at in range(0, w_all, 256):
                w = min(256, w_all - at)
                cols = ring[ch][:, :, at : at + w].reshape(NZ * tok, w)
                stage[ch][peer, :, at : at + w] = jnp.dot(rows, cols, preferred_element_type=F32).astype(BF16)

            @pl.when(peer != me)
            def _():
                for copy in x_copies(ch, peer, me, me):
                    copy.start()

            @pl.when(peer == me)
            def _():
                for copy in own_copies(ch):
                    copy.start()

            return 0

        lax.fori_loop(lo, hi, one, 0)

    per_x = NZ * NC * cap
    new = lax.broadcasted_iota(jnp.int32, (unit, per_x), 0)
    old = lax.broadcasted_iota(jnp.int32, (unit, per_x), 1)
    core = (new >= padded).astype(jnp.int32)
    inner = new - core * padded

    def prepare(b):
        order = jnp.zeros((unit, per_x), jnp.bool_)
        for zed in range(NZ):
            order = order | (
                (inner >= zed * cap) & (inner < (zed + 1) * cap) & (old == inner + zed * (NC - 1) * cap + core * cap)
            )
        moved = jnp.dot(order.astype(F32).astype(BF16), saved[aligned(b, per_x), :], preferred_element_type=F32)
        gate, lift = moved[:, :hidden], moved[:, hidden:]
        sig = jax.nn.sigmoid(gate)
        rows = aligned(b, unit)
        swish = gate * sig
        act[rows, :] = (swish * lift).astype(BF16)
        coef_gate[rows, :] = lift * sig * (1.0 + gate * (1.0 - sig))
        coef_up[rows, :] = swish

    def gain_of(b):
        side = side_rows[pl.ds(b * NC, NC), :, :].reshape(unit, LANES).astype(F32)
        mine = expert.astype(F32)
        gain = jnp.zeros((unit, 1), F32)
        for k in range(TOP):
            gain = gain + jnp.where(side[:, k : k + 1] == mine, side[:, GATE_LANE + k : GATE_LANE + k + 1], 0.0)
        return side, mine, gain

    def scale_rows(b):
        two = pl.ds(b * NC, NC)
        gain = gain_of(b)[2]
        for at in range(0, width, 512):
            part = dy_rows[two, :, at : at + 512].reshape(unit, 512).astype(F32)
            scaled_rows[two, :, at : at + 512] = (gain * part).astype(BF16).reshape(NC, padded, 512)

    def pre_copy(b):
        rows = aligned(b, unit)
        return pltpu.make_async_copy(pre_out.at[rows, :], pre_hbm.at[rows, :], w_sem.at[0, b])

    def row_copy(b):
        two = pl.ds(b * NC, NC)
        return pltpu.make_async_copy(row_out.at[two], row_hbm.at[two], w_sem.at[1, b])

    def through_down(b):
        rows = aligned(b, unit)
        two = pl.ds(b * NC, NC)
        dy = dy_rows[two, :, :].reshape(unit, width)
        act_grad = lax.dot_general(dy, down[...].reshape(hidden, width), NT, preferred_element_type=F32)
        gate_grad = jnp.sum(act[rows, :].astype(F32) * act_grad, axis=1, keepdims=True) / jnp.sqrt(F32(width))
        side, mine, gain = gain_of(b)
        lane = lax.broadcasted_iota(jnp.int32, (unit, LANES), 1)
        gate_out[two, :, :] = (
            jnp.where((lane < TOP) & (side == mine), jnp.broadcast_to(gate_grad, (unit, LANES)), 0.0)
            .astype(BF16)
            .reshape(NC, padded, LANES)
        )
        scaled = gain * act_grad
        pre_out[rows, 0:hidden] = (scaled * coef_gate[rows, :]).astype(BF16)
        pre_out[rows, hidden : 2 * hidden] = (scaled * coef_up[rows, :]).astype(BF16)
        pre_copy(b).start()

    def through_up(b):
        rows = aligned(b, unit)
        two = pl.ds(b * NC, NC)

        def one(q, _):
            grad = lax.dot_general(pre_out[rows, :], up[q], NT, preferred_element_type=F32)
            row_out[two, :, aligned(q, up.shape[1])] = grad.astype(BF16).reshape(NC, padded, up.shape[1])
            return 0

        lax.fori_loop(0, NY, one, 0)
        row_copy(b).start()

    def down_grad(k):
        cols = aligned(k, 512)
        scaled_dy = scaled_rows[:, :, cols].reshape(PEERS * padded, 512)
        dn[:, :, cols] = (
            jnp.dot(turned_act[...], scaled_dy, preferred_element_type=F32).astype(BF16).reshape(NY, hidden // NY, 512)
        )

    dn_rows = hidden // NY
    dn_cut = dn_rows // 32 * 16
    spans = ((0, dn_cut), (dn_cut, dn_rows - dn_cut))

    def dn_hop(k):
        lo, size = spans[(0, 1, 0, 1, 0, 1)[k]]
        src = dn_sum.at[k // 3, 0:size, :]
        if k in (0, 1, 3, 4):
            ahead = (2, 1, 0, 2, NY - 1)[k]
            src = dn.at[lax.rem(y + ahead, NY), lo : lo + size, :]
        return pltpu.make_async_remote_copy(
            src_ref=src,
            dst_ref=dn_come.at[k, 0:size, :],
            send_sem=d_send.at[k],
            recv_sem=d_recv.at[k],
            device_id=along_y(1 if k < 3 else NY - 1),
            device_id_type=MESH,
        )

    def dn_pass_on():
        for k in (2, 5):
            lo, size = spans[0 if k == 2 else 1]
            dn_hop(k - 2).wait_recv()
            own = dn[lax.rem(y + (1 if k == 2 else NY - 1), NY), lo : lo + size, :].astype(F32)
            dn_sum[k // 3, 0:size, :] = (own + dn_come[k - 2, 0:size, :].astype(F32)).astype(BF16)
            dn_hop(k).start()

    def dn_finish():
        for (lo, size), (a, b) in zip(spans, ((2, 4), (1, 5))):
            dn_hop(a).wait_recv()
            dn_hop(b).wait_recv()
            value = dn[y, lo : lo + size, :].astype(F32)
            value = value + dn_come[a, 0:size, :].astype(F32) + dn_come[b, 0:size, :].astype(F32)
            dn_out[lo : lo + size, :] = value * scale

    def run(work, lo, hi):
        def one(b, _):
            work(b)
            return 0

        lax.fori_loop(lo, hi, one, 0)

    for k in (0, 1):
        y_own_copy(k).start()
        for h in (0, 2, 1, 3):
            y_copy(k, h).start()
    ticks = sends - 2
    half_n = n // 2

    def drained(ch):
        def sent(step, _):
            peer = lax.rem(me + step, PEERS)
            for copy in x_copies(ch, peer, me, me):
                copy.wait_send()
            return 0

        lax.fori_loop(1, PEERS, sent, 0)

    def own_landed(ch):
        for copy in own_copies(ch):
            copy.wait()

    def free_stage(ch):
        if ch >= half_n:
            drained(ch - half_n)

    def x_landed(ch):
        def one(step, _):
            peer = lax.rem(me + step, PEERS)
            for copy in x_copies(ch, peer, peer, peer):
                copy.wait_recv()
            return 0

        lax.fori_loop(1, PEERS, one, 0)

    z_start(0, 0)
    z_start(0, 1)
    for ch in range(n):
        if ch > 0:
            z_arrived(ch - 1, sends - 2)
            z_arrived(ch - 1, sends - 1)
            free_stage(ch - 1)
        if ch > 1:
            own_landed(ch - 2)
        if ch == 1:
            make_pick()
        if ch in (2, 3):
            y_forward(ch - 2)

        def tick(i, _, ch=ch):
            z_arrived(ch, i)
            z_start(ch, i + 2)
            if ch + 1 < n:

                @pl.when(i >= ticks - 2)
                def _():
                    z_start(ch + 1, i - (ticks - 2))

            if ch == 0:
                run(prepare, (NX * i) // ticks, (NX * (i + 1)) // ticks)
            else:
                pieces(ch - 1, jnp.minimum(4 * i, PEERS), jnp.minimum(4 * i + 4, PEERS))
            if ch == half_n + 1:

                @pl.when(i == 2)
                def _():
                    for k in range(half_n):
                        x_landed(k)
                    run(scale_rows, 0, NX)

                tiles = width // 512
                run(down_grad, jnp.clip(2 * (i - 3), 0, tiles), jnp.clip(2 * (i - 2), 0, tiles))
            if ch == n - 1:

                @pl.when(i == 0)
                def _():
                    y_arrived(0)

                run(through_down, jnp.maximum(i - 1, 0), i)
            return 0

        lax.fori_loop(0, ticks, tick, 0)
        if ch == 0:
            turned_act[...] = act[...].astype(F32).T.astype(BF16)
        if ch == half_n + 1:
            for k in (0, 3, 1, 4):
                dn_hop(k).start()
    z_arrived(n - 1, sends - 2)
    z_arrived(n - 1, sends - 1)
    free_stage(n - 1)
    pieces(n - 1, 0, PEERS)
    dn_pass_on()
    y_arrived(1)
    run(through_up, 0, NX)
    dn_finish()
    for ch in range(n):
        if ch >= half_n:
            x_landed(ch)
            drained(ch)
        if ch >= n - 2:
            own_landed(ch)

        def drain(i, _, ch=ch):
            for way in (0, 1):
                hop(ch, way, i).wait_send()
            return 0

        lax.fori_loop(0, sends, drain, 0)
    for b in range(NX):
        pre_copy(b).wait()
        row_copy(b).wait()
    for k in (0, 1):
        for h in range(6):
            y_copy(k, h).wait_send()
    for k in range(6):
        dn_hop(k).wait_send()


def front(side, dy, x, saved, up, down, cap, scale):
    tok, width = dy.shape
    hidden = up.shape[1] // 2
    block = NZ * cap
    padded = -(-block // 16) * 16
    chunks = []
    for array, widths in ((1, DY_CHUNKS), (2, X_CHUNKS)):
        col = 0
        for w in widths:
            off = 0 if chunks else LANES
            chunks.append(([(0, 0, LANES, 0)] * (off > 0) + [(array, col, w, off)], off + w))
            col += w
    n = len(chunks)
    rows = PEERS * padded
    dn_part = hidden // NY - hidden // NY // 32 * 16
    vmem = pl.BlockSpec(memory_space=pltpu.VMEM)
    anywhere = pl.BlockSpec(memory_space=pl.ANY)
    shape = jax.ShapeDtypeStruct
    return pl.pallas_call(
        functools.partial(front_kernel, chunks, cap, scale),
        out_shape=(
            shape((NZ, tok, LANES), BF16),
            shape((PEERS, padded, width), BF16),
            shape((rows, 2 * hidden), BF16),
            shape((PEERS, padded, LANES), BF16),
            shape((PEERS, padded, width), BF16),
            shape((hidden // NY, width), F32),
        ),
        in_specs=[vmem] * 4 + [anywhere] * 2,
        out_specs=(vmem, anywhere, anywhere, vmem, anywhere, vmem),
        scratch_shapes=[pltpu.VMEM((NZ, tok, w), BF16) for _, w in chunks]
        + [pltpu.VMEM((PEERS, block, max(a[1], b[1])), BF16) for a, b in zip(chunks[: n // 2], chunks[n // 2 :])]
        + [
            pltpu.VMEM((tok, LANES), BF16),
            pltpu.VMEM((PEERS, padded, LANES), BF16),
            pltpu.VMEM((PEERS, padded, width), BF16),
            pltpu.VMEM((PEERS, padded, width), BF16),
            pltpu.VMEM((PEERS, block, NZ * tok), BF16),
            pltpu.VMEM((NY,) + up.shape, BF16),
            pltpu.VMEM((NY,) + down.shape, BF16),
            pltpu.VMEM((rows, hidden), BF16),
            pltpu.VMEM((hidden, rows), BF16),
            pltpu.VMEM((rows, hidden), F32),
            pltpu.VMEM((rows, hidden), F32),
            pltpu.VMEM((NY, hidden // NY, width), BF16),
            pltpu.VMEM((6, dn_part, width), BF16),
            pltpu.VMEM((2, dn_part, width), BF16),
            pltpu.VMEM((rows, 2 * hidden), BF16),
            pltpu.VMEM((PEERS, padded, width), BF16),
            pltpu.SemaphoreType.DMA((n, 2, NZ - 1)),
            pltpu.SemaphoreType.DMA((n, 2, NZ - 1)),
            pltpu.SemaphoreType.DMA((n, 2, PEERS)),
            pltpu.SemaphoreType.DMA((n, 2, PEERS)),
            pltpu.SemaphoreType.DMA((n, 2)),
            pltpu.SemaphoreType.DMA((2, 6)),
            pltpu.SemaphoreType.DMA((2, 6)),
            pltpu.SemaphoreType.DMA((2,)),
            pltpu.SemaphoreType.DMA((6,)),
            pltpu.SemaphoreType.DMA((6,)),
            pltpu.SemaphoreType.DMA((2, NX)),
        ],
        compiler_params=pltpu.CompilerParams(collective_id=0, has_side_effects=True, vmem_limit_bytes=62 << 20),
        cost_estimate=pl.CostEstimate(flops=20_000_000_000, bytes_accessed=350_000_000, transcendentals=0),
        name="front",
    )(side, dy, x, saved, up, down)


def back_kernel(
    chunks, cap, scale, side_ref, gate_ref, row_ref, x_hbm, pre_hbm, gate_out, tok_out, gu_out, *scratch
):
    n = len(chunks)
    landed, total, leave, come = (scratch[k * n : (k + 1) * n] for k in range(4))
    spread, gu_leave, gu_come, x_ref, pre_ref, z_send, z_recv, x_send, x_recv, own_sem, y_send, y_recv, in_sem = scratch[4 * n :]
    ins, outs = (gate_ref, row_ref), (gate_out, tok_out)
    x, z, c = place()
    y = lax.axis_index("dp")
    me = x * NC + c
    tok = tok_out.shape[0]
    half_rows = tok // 2
    block = NZ * cap
    padded = row_ref.shape[1]
    pad = landed[0].shape[1]
    sends = NZ - 1

    x_ref[:, block:, :] = jnp.zeros((PEERS, padded - block, x_ref.shape[2]), BF16)
    fetches = (
        pltpu.make_async_copy(x_hbm.at[:, 0:block, :], x_ref.at[:, 0:block, :], in_sem.at[0]),
        pltpu.make_async_copy(pre_hbm, pre_ref, in_sem.at[1]),
    )
    for copy in fetches:
        copy.start()
    for buf, (_, w) in zip(landed, chunks):
        buf[:, block:, :] = jnp.zeros((PEERS, pad - block, w), BF16)
    enter(x, z, c)

    def x_copies(ch, src_slot, dst_slot, mark, peer):
        made = []
        for array, col, w, off in chunks[ch][0]:
            made.append(
                pltpu.make_async_remote_copy(
                    src_ref=ins[array].at[src_slot, 0:block, col : col + w],
                    dst_ref=landed[ch].at[dst_slot, 0:block, off : off + w],
                    send_sem=x_send.at[ch, array, peer],
                    recv_sem=x_recv.at[ch, array, mark],
                    device_id=device(peer // NC, z, lax.rem(peer, NC)),
                    device_id_type=MESH,
                )
            )
        return made

    def own_copies(ch):
        return [
            pltpu.make_async_copy(
                ins[array].at[me, 0:block, col : col + w], landed[ch].at[me, 0:block, off : off + w], own_sem.at[ch, array]
            )
            for array, col, w, off in chunks[ch][0]
        ]

    def x_start(ch):
        def send(step, _):
            peer = lax.rem(me + step, PEERS)
            for copy in x_copies(ch, peer, me, me, peer):
                copy.start()
            return 0

        lax.fori_loop(1, PEERS, send, 0)
        for copy in own_copies(ch):
            copy.start()

    x_start(0)
    x_start(1)

    gu_rows = gu_out.shape[0]
    half_gu = gu_rows // 2

    def gu_part(ahead, half):
        first = lax.rem(y + ahead, NY) * gu_rows + half * half_gu
        cols = x_ref[:, :, pl.ds(pl.multiple_of(first, half_gu), half_gu)].reshape(PEERS * padded, half_gu)
        return lax.dot_general(cols, pre_ref[...], TN, preferred_element_type=F32)

    def gu_hop(k):
        return pltpu.make_async_remote_copy(
            src_ref=gu_leave.at[k],
            dst_ref=gu_come.at[k],
            send_sem=y_send.at[k],
            recv_sem=y_recv.at[k],
            device_id=along_y(1 if k < 3 else NY - 1),
            device_id_type=MESH,
        )

    def gu_send(k):
        up = k < 3
        ahead = 2 if k in (0, 3) else (1 if up else NY - 1)
        half = (0 if up else 1) if k in (0, 2, 3, 5) else (1 if up else 0)
        value = gu_part(ahead, half)
        if k in (2, 5):
            gu_hop(k - 2).wait_recv()
            value = value + gu_come[k - 2].astype(F32)
        gu_leave[k] = value.astype(BF16)
        gu_hop(k).start()

    def gu_own(half):
        gu_out[half * half_gu : (half + 1) * half_gu, :] = gu_part(0, half)

    def gu_finish():
        for half in (0, 1):
            rows = slice(half * half_gu, (half + 1) * half_gu)
            a, b = (2, 4) if half == 0 else (1, 5)
            gu_hop(a).wait_recv()
            gu_hop(b).wait_recv()
            gu_out[rows, :] = (gu_out[rows, :] + gu_come[a].astype(F32) + gu_come[b].astype(F32)) * scale

    for copy in fetches:
        copy.wait()
    gu_send(0)
    gu_send(3)

    later = (
        lax.broadcasted_iota(jnp.int32, (tok, tok), 1) < lax.broadcasted_iota(jnp.int32, (tok, tok), 0)
    ).astype(BF16)
    lane = lax.broadcasted_iota(jnp.int32, (tok, LANES), 1)
    expert_lane = jnp.where(lane < PEERS, (lane // NC) * (NZ * NC) + z * NC + lax.rem(lane, NC), -1).astype(F32)
    slot_lane = lax.broadcasted_iota(jnp.int32, (tok, pad), 1).astype(F32)

    def spread_one(s, _):
        side = side_ref[s].astype(F32)
        match = jnp.zeros((tok, LANES), F32)
        for k in range(TOP):
            match = match + (jnp.broadcast_to(side[:, k : k + 1], (tok, LANES)) == expert_lane).astype(F32)
        position = jnp.dot(later, match.astype(BF16), preferred_element_type=F32)
        slot = jnp.where(match > 0.0, position + (s * cap).astype(F32), -1.0)
        for peer in range(PEERS):
            hit = jnp.broadcast_to(slot[:, peer : peer + 1], (tok, pad)) == slot_lane
            spread[s, :, peer * pad : (peer + 1) * pad] = hit.astype(F32).astype(BF16)
        return 0

    lax.fori_loop(0, NZ, spread_one, 0)

    def x_arrived(ch):
        def one(step, _):
            peer = lax.rem(me + step, PEERS)
            for copy in x_copies(ch, peer, peer, peer, peer):
                copy.wait_recv()
            return 0

        lax.fori_loop(1, PEERS, one, 0)
        for copy in own_copies(ch):
            copy.wait()

    def combines(ch, lo, hi):
        def one(k, _):
            width = chunks[ch][1]
            s = lax.rem(z + NZ // 2 + k, NZ)
            rows = spread[s]
            for at in range(0, width, 256):
                w = min(256, width - at)
                cols = landed[ch][:, :, at : at + w].reshape(PEERS * pad, w)
                total[ch][s, :, at : at + w] = jnp.dot(rows, cols, preferred_element_type=F32)
            return 0

        lax.fori_loop(lo, hi, one, 0)

    def hop(ch, way, i):
        step = 1 + way * (NZ - 2)
        return pltpu.make_async_remote_copy(
            src_ref=leave[ch].at[way, i],
            dst_ref=come[ch].at[way, i],
            send_sem=z_send.at[ch, way, i],
            recv_sem=z_recv.at[ch, way, i],
            device_id=device(x, lax.rem(z + step, NZ), c),
            device_id_type=MESH,
        )

    def z_step(ch, i):
        dist = NZ // 2 - (i + 1) // 2

        def one(way, _):
            s = lax.rem(z + (1 + way * (NZ - 2)) * dist, NZ)
            half = lax.rem(i + way, 2)
            value = total[ch][s, aligned(half, half_rows), :]
            if i >= 2:
                hop(ch, way, i - 2).wait_recv()
                value = value + come[ch][way, i - 2].astype(F32)
            leave[ch][way, i] = value.astype(BF16)
            hop(ch, way, i).start()
            return 0

        lax.fori_loop(0, 2, one, 0)

    def finish(ch):
        for way in (0, 1):
            hop(ch, way, sends - 2).wait_recv()
            hop(ch, way, sends - 1).wait_recv()
        for half in (0, 1):
            rows = slice(half * half_rows, (half + 1) * half_rows)
            value = total[ch][z, rows, :]
            for way in (0, 1):
                i = sends - 1 if (sends - 1 + way) % 2 == half else sends - 2
                value = value + come[ch][way, i].astype(F32)
            for array, col, w, off in chunks[ch][0]:
                outs[array][rows, col : col + w] = value[:, off : off + w].astype(BF16)

    x_start(2)
    x_arrived(0)
    combines(0, 0, NZ)
    period = NZ // 2
    extra = {
        0: ((gu_send, 1), (gu_send, 4)),
        1: ((gu_send, 2), (gu_send, 5)),
        2: ((gu_own, 0), (gu_own, 1)),
    }
    for tick in range(period * (n - 1) + sends):
        ch, r = divmod(tick, period)
        for k, i in ((ch - 1, r + period), (ch, r)):
            if 0 <= k < n and i < sends:
                z_step(k, i)
        if ch < n:
            if r == 0 and ch + 1 < n:
                x_arrived(ch + 1)
                if ch + 3 < n:
                    x_start(ch + 3)
            if ch + 1 < n:
                combines(ch + 1, NZ * r // period, NZ * (r + 1) // period)
            if r == 1 and ch > 1:
                finish(ch - 2)
            if r in (1, 3) and ch in extra:
                work, arg = extra[ch][r // 2]
                work(arg)
    finish(n - 2)
    finish(n - 1)
    gu_finish()
    for ch in range(n):

        def drain(i, _, ch=ch):
            for way in (0, 1):
                hop(ch, way, i).wait_send()
            return 0

        lax.fori_loop(0, sends, drain, 0)

        def sent(step, _, ch=ch):
            peer = lax.rem(me + step, PEERS)
            for copy in x_copies(ch, peer, me, me, peer):
                copy.wait_send()
            return 0

        lax.fori_loop(1, PEERS, sent, 0)
    for k in range(6):
        gu_hop(k).wait_send()


def back(side, gate_rows, rows, x_rows, pre, cap, gu_rows, scale):
    width = rows.shape[2]
    tok = side.shape[1]
    pad = -(-NZ * cap // LANES) * LANES
    chunks, col = [], 0
    for w in BACK_CHUNKS:
        off = 0 if chunks else LANES
        chunks.append(([(0, 0, LANES, 0)] * (off > 0) + [(1, col, w, off)], off + w))
        col += w
    n = len(chunks)
    vmem = pl.BlockSpec(memory_space=pltpu.VMEM)
    shape = jax.ShapeDtypeStruct
    return pl.pallas_call(
        functools.partial(back_kernel, chunks, cap, scale),
        out_shape=(shape((tok, LANES), BF16), shape((tok, width), BF16), shape((gu_rows, pre.shape[1]), F32)),
        in_specs=[vmem, vmem] + [pl.BlockSpec(memory_space=pl.ANY)] * 3,
        out_specs=(vmem,) * 3,
        scratch_shapes=[pltpu.VMEM((PEERS, pad, w), BF16) for _, w in chunks]
        + [pltpu.VMEM((NZ, tok, w), F32) for _, w in chunks]
        + [pltpu.VMEM((2, NZ - 1, tok // 2, w), BF16) for _, w in chunks] * 2
        + [
            pltpu.VMEM((NZ, tok, PEERS * pad), BF16),
            pltpu.VMEM((6, gu_rows // 2, pre.shape[1]), BF16),
            pltpu.VMEM((6, gu_rows // 2, pre.shape[1]), BF16),
            pltpu.VMEM(x_rows.shape, BF16),
            pltpu.VMEM(pre.shape, BF16),
            pltpu.SemaphoreType.DMA((n, 2, NZ - 1)),
            pltpu.SemaphoreType.DMA((n, 2, NZ - 1)),
            pltpu.SemaphoreType.DMA((n, 2, PEERS)),
            pltpu.SemaphoreType.DMA((n, 2, PEERS)),
            pltpu.SemaphoreType.DMA((n, 2)),
            pltpu.SemaphoreType.DMA((6,)),
            pltpu.SemaphoreType.DMA((6,)),
            pltpu.SemaphoreType.DMA((2,)),
        ],
        compiler_params=pltpu.CompilerParams(collective_id=1, has_side_effects=True, vmem_limit_bytes=47 << 20),
        cost_estimate=pl.CostEstimate(flops=10_000_000_000, bytes_accessed=250_000_000, transcendentals=0),
        name="back",
    )(side, gate_rows, rows, x_rows, pre)


def on_device(tokens, out_grad, routes, gate_weights, saved_preacts, gate_up, down_proj):
    groups = lax.axis_size("dp")
    tok_rows, top = routes.shape
    cap = saved_preacts.shape[2] // lax.axis_size("expert")
    zeros = functools.partial(jnp.zeros, dtype=BF16)
    side = jnp.concatenate(
        [
            routes.T.astype(BF16),
            zeros((GATE_LANE - top, tok_rows)),
            gate_weights.T,
            zeros((LANES - GATE_LANE - top, tok_rows)),
        ]
    )
    grad_scale = float(1.0 / (groups * tok_rows * top) ** 0.5)
    sides, x_rows, pre, gate_rows, rows, grad_dn = front(
        side, out_grad, tokens, saved_preacts[0, 0], gate_up[0], down_proj[0], cap, grad_scale
    )
    gates, grad_tokens, grad_gu = back(sides, gate_rows, rows, x_rows, pre, cap, gate_up.shape[1], grad_scale)
    return (grad_tokens, gates[:, :top], grad_gu[None], grad_dn[None])


def solution(mesh):
    in_specs = (
        P(("dp", "expert"), None),
        P(("dp", "expert"), None),
        P(("dp", "expert"), None),
        P(("dp", "expert"), None),
        P("dp", "expert", None, None),
        P("expert", "dp", None),
        P("expert", "dp", None),
    )
    out_specs = (
        P(("dp", "expert"), None),
        P(("dp", "expert"), None),
        P("expert", "dp", None),
        P("expert", "dp", None),
    )
    return jax.shard_map(
        on_device, mesh=mesh, in_specs=in_specs, out_specs=out_specs, check_vma=False
    )
```
